32 devices in a mesh: wave: 8 (over z, core), lev: 4 (over y, x).
Axes of the slice: x: 2, y: 2, z: 4, core: 2. Of those that a mesh axis runs over, the one named last changes fastest.
Arguments:
- spectrum: bfloat16 [4, 4, 2, 1280, 1280], P(None, 'lev', None, 'wave'), may hold values from -6 to 6
- legendre: bfloat16 [1280, 8, 1280], P('wave'), may hold values from -0.15625 to 0.15625
- order_of_slot: int32 [1280], replicated, may hold values from 0 to 1279, each once
- reduced_length: int32 [8], replicated, may hold values from 20 to 5136, as said below
- gauss_weight: float32 [8], P('wave'), may hold values from 2 to 6
- depart_row: int32 [2, 4, 4, 8, 5632], P(None, 'lev', None, 'wave'), may hold values from -1 to 1, as said below
- depart_col: int32 [2, 4, 4, 8, 5632], P(None, 'lev', None, 'wave'), may hold values from 0 to 5135, as said below
- depart_weight: float32 [2, 4, 4, 8, 5632], P(None, 'lev', None, 'wave'), may hold values from 0.05 to 0.5
Outputs:
- spectrum_out: bfloat16 [4, 4, 2, 1280, 1280], P(None, 'lev', None, 'wave')
The draws below stay inside these ranges and needn't reach their ends.
Inputs may be any that keep to these rules, and one draw needn't show every extreme that they name: `reduced_length`: each latitude j has 20 + 4 i points for a cycle i with j * 160 <= i < (j + 1) * 160; the last latitude has 5136. `depart_row`: offset of the departure latitude from the arrival latitude; a departure latitude outside the window reads zeros. `depart_col`: below the reduced length of the departure latitude (of the nearest window latitude where it lies outside the window). `order_of_slot`: A permutation of the zonal orders.
All inputs are finite; a program needn't handle non-finite values.
Results may differ from the reference program's by a relative error of at most 0.02.
Values may be sent and summed in bfloat16 or wider, within the bound.
A program may use at most 128 MiB of HBM per device.

```python
import math
import jax
import jax.numpy as jnp
from jax import lax

ORDERS = 1280
VARS = 4
STEPS = 2
STENCIL = 4
BLOCK = 512
LAT = 8
LEVELS = 4
GRID = 5632


def cycle_lengths(key):
    stride = ORDERS // LAT
    cycle_offset = jax.random.randint(jax.random.fold_in(key, 11), (LAT,), 0, stride)
    cycle_index = jnp.arange(LAT, dtype=jnp.int32) * stride + cycle_offset
    cycle_index = cycle_index.at[LAT - 1].set(ORDERS - 1)
    return (20 + 4 * cycle_index).astype(jnp.int32)


def offsets_of(key):
    array_shape = (STEPS, LEVELS, STENCIL, LAT, GRID)
    offsets = jax.random.randint(jax.random.fold_in(key, 12), array_shape, -1, 2)
    offsets = offsets.at[..., 0].set(0).at[..., 1].set(-1).at[..., 2].set(1)
    return offsets.astype(jnp.int32)


def draw_reduced_length(key, part):
    return cycle_lengths(key)


def draw_depart_row(key, part):
    return offsets_of(key)


def draw_depart_col(key, part):
    array_shape = (STEPS, LEVELS, STENCIL, LAT, GRID)
    lengths = cycle_lengths(key)
    offsets = offsets_of(key)
    target = jnp.clip(jnp.arange(LAT, dtype=jnp.int32)[:, None] + offsets, 0, LAT - 1)
    row_length = lengths[target]
    fraction = jax.random.randint(jax.random.fold_in(key, 13), array_shape, 0, 262144)
    columns = fraction * row_length // 262144
    columns = columns.at[..., 0].set(row_length[..., 0] - 1)
    return columns.astype(jnp.int32)


def steps_of(own_key, dims, split, smallest, largest):
    def one(position, blocks):
        draws = jax.random.uniform(jax.random.fold_in(jax.random.fold_in(own_key, 6), position), (blocks,), jnp.float32, smallest / len(split), largest / len(split))
        return jnp.repeat(jnp.exp(draws), dims[position] // blocks).reshape((-1,) + (1,) * (len(dims) - position - 1))

    gain = one(*split[0])
    for cut in split[1:]:
        gain = gain * one(*cut)
    return gain


def bell_draw(own_key, extent, width, reach, cuts=(), kind=jnp.bfloat16):
    level = steps_of(own_key, extent, cuts, -0.22, 0.18) if cuts else 1.0
    array = jax.random.normal(own_key, extent, jnp.float32) * width * level
    return jnp.minimum(jnp.maximum(array, -reach), reach).astype(kind)


def setup_inputs(seed: int = 0) -> dict:
    arg_keys = jax.random.split(jax.random.key(seed), 9)
    return {
        "spectrum": bell_draw(arg_keys[0], (VARS, LEVELS, 2, ORDERS, ORDERS), 1.0, 6.0, ((1, 4), (3, 8))),
        "legendre": bell_draw(arg_keys[1], (ORDERS, LAT, ORDERS), ORDERS ** -0.5, 0.15625, ((0, 8),)),
        "order_of_slot": jax.random.permutation(arg_keys[2], ORDERS).astype(jnp.int32),
        "reduced_length": draw_reduced_length(jax.random.fold_in(arg_keys[8], 71), 0),
        "gauss_weight": jnp.clip(2.0 + 4.0 * jax.random.uniform(arg_keys[4], (LAT,), jnp.float32) ** steps_of(arg_keys[4], (LAT,), ((0, 8),), -0.2, 0.2), 2.0, 6.0),
        "depart_row": draw_depart_row(jax.random.fold_in(arg_keys[8], 71), 0),
        "depart_col": draw_depart_col(jax.random.fold_in(arg_keys[8], 71), 0),
        "depart_weight": jnp.clip(0.05 + 0.45 * jax.random.uniform(arg_keys[7], (STEPS, LEVELS, STENCIL, LAT, GRID), jnp.float32) ** steps_of(arg_keys[7], (STEPS, LEVELS, STENCIL, LAT, GRID), ((1, 4), (3, 8)), -0.2, 0.2), 0.05, 0.5),
    }


full_turn = 2.0 * math.pi

def base_table(length, orders, order_limit):
    offsets = jnp.arange(BLOCK, dtype=jnp.int32)
    phases = orders[:, None] * offsets[None, :] % length
    angles = phases.astype(jnp.float32) * (jnp.float32(full_turn) / length.astype(jnp.float32))
    active = (orders < order_limit)[:, None]
    cosine = jnp.where(active, jnp.cos(angles), 0.0)
    sine_part = jnp.where(active, -jnp.sin(angles), 0.0)
    return jnp.concatenate([cosine, sine_part], axis=0).astype(jnp.bfloat16)

def block_phases(length, orders):
    starts = jnp.arange(GRID // BLOCK, dtype=jnp.int32) * BLOCK
    phases = starts[:, None] * orders[None, :] % length
    angles = phases.astype(jnp.float32) * (jnp.float32(full_turn) / length.astype(jnp.float32))
    return (jnp.cos(angles), jnp.sin(angles))

def synthesize(coeffs, length, order_limit, fourier_table, cos_phase, sin_phase):
    field_count = coeffs.shape[0]
    blocks = cos_phase.shape[0]
    real_part = coeffs[:, 0, :].astype(jnp.float32)[:, None, :]
    imag_part = coeffs[:, 1, :].astype(jnp.float32)[:, None, :]
    rot_real = real_part * cos_phase[None] - imag_part * sin_phase[None]
    rot_imag = real_part * sin_phase[None] + imag_part * cos_phase[None]
    rotated = jnp.stack([rot_real, rot_imag], axis=2).astype(jnp.bfloat16)
    rotated = rotated.reshape(field_count * blocks, -1)
    result = jnp.dot(rotated.astype(jnp.float32), fourier_table.astype(jnp.float32), preferred_element_type=jnp.float32)
    result = result.reshape(field_count, blocks * BLOCK)
    points = jnp.arange(blocks * BLOCK, dtype=jnp.int32)
    factor = 1.0 / jnp.sqrt(order_limit.astype(jnp.float32))
    return jnp.where(points[None, :] < length, result * factor, 0.0)

def analyse(newgrid, fourier_table, cos_phase, sin_phase):
    field_count = newgrid.shape[0]
    blocks = cos_phase.shape[0]
    partial_value = jnp.dot(newgrid.reshape(field_count * blocks, BLOCK).astype(jnp.float32), fourier_table.astype(jnp.float32).T, preferred_element_type=jnp.float32)
    partial_value = partial_value.reshape(field_count, blocks, 2, -1)
    part_real = partial_value[:, :, 0, :]
    part_imag = partial_value[:, :, 1, :]
    real_sum = lax.optimization_barrier(jnp.sum(part_real * cos_phase[None] + part_imag * sin_phase[None], axis=1))
    imag_sum = lax.optimization_barrier(jnp.sum(part_imag * cos_phase[None] - part_real * sin_phase[None], axis=1))
    return jnp.stack([real_sum, imag_sum], axis=1)

def reference(spectrum, legendre, order_of_slot, reduced_length, gauss_weight, depart_row, depart_col, depart_weight):
    degrees = jnp.arange(ORDERS, dtype=jnp.int32)
    masked = jnp.where(degrees[None, None, :] >= order_of_slot[:, None, None], legendre.astype(jnp.float32), 0.0)
    limits = jnp.minimum(ORDERS, (reduced_length - 1) // 2)
    latitudes = jnp.arange(LAT, dtype=jnp.int32)
    points = jnp.arange(GRID, dtype=jnp.int32)
    field_count = VARS * LEVELS
    spectral_state = spectrum

    def synth_level(level_state):
        return jnp.einsum('vcsn,sjn->jvcs', level_state.astype(jnp.float32), masked).astype(jnp.bfloat16)

    def analyse_level(level_coeffs):
        return jnp.einsum('jvcs,sjn->vcsn', level_coeffs.astype(jnp.float32), masked).astype(jnp.bfloat16)

    def grid_of(mapped):
        coeffs, length, order_limit = mapped
        fourier_table = base_table(length, order_of_slot, order_limit)
        cos_phase, sin_phase = block_phases(length, order_of_slot)
        return synthesize(coeffs, length, order_limit, fourier_table, cos_phase, sin_phase)

    def coeffs_of(mapped):
        rows_grid, length, order_limit, weight = mapped
        fourier_table = base_table(length, order_of_slot, order_limit)
        cos_phase, sin_phase = block_phases(length, order_of_slot)
        sums = analyse(rows_grid, fourier_table, cos_phase, sin_phase)
        return (sums * (weight * jnp.sqrt(2.0 / length.astype(jnp.float32)))).astype(jnp.bfloat16)

    def interp_level(mapped):
        flat_rows, row_offsets, columns, weights = mapped
        flat_index = (latitudes[None, :, None] + 1 + row_offsets) * GRID + columns
        values = flat_rows[:, flat_index.reshape(-1)].reshape(VARS, STENCIL, LAT, GRID)
        return lax.optimization_barrier(jnp.sum(values * weights[None], axis=1))
    for step_index in range(STEPS):
        fourier = lax.map(synth_level, jnp.moveaxis(spectral_state, 1, 0))
        fourier = jnp.transpose(fourier, (1, 2, 0, 3, 4)).reshape(LAT, field_count, 2, ORDERS)
        gridpoints = lax.map(grid_of, (fourier, reduced_length, limits))
        gridpoints = jnp.transpose(gridpoints.reshape(LAT, VARS, LEVELS, GRID), (2, 1, 0, 3))
        padded = jnp.pad(gridpoints, ((0, 0), (0, 0), (1, 1), (0, 0))).reshape(LEVELS, VARS, (LAT + 2) * GRID)
        interp = lax.map(interp_level, (padded, depart_row[step_index], depart_col[step_index], depart_weight[step_index]))
        tendency = interp + 0.5 * jnp.roll(interp, -1, axis=1) * jnp.tanh(jnp.roll(interp, -2, axis=1))
        newgrid = jnp.where(points[None, None, None, :] < reduced_length[None, None, :, None], tendency, 0.0).astype(jnp.bfloat16)
        newgrid = jnp.transpose(newgrid, (2, 1, 0, 3)).reshape(LAT, field_count, GRID)
        coeffs = lax.map(coeffs_of, (newgrid, reduced_length, limits, gauss_weight))
        coeffs = coeffs.reshape(LAT, VARS, LEVELS, 2, ORDERS)
        spectral_state = jnp.moveaxis(lax.map(analyse_level, jnp.moveaxis(coeffs, 2, 0)), 0, 1)
    return spectral_state
```

```python
import functools
import math

import jax
import jax.numpy as jnp
from jax import lax
from jax.experimental import pallas as pl
from jax.experimental.pallas import tpu as pltpu
from jax.sharding import PartitionSpec as P

BLOCK = 512
RADIX = 8
FULL_TURN = 2.0 * math.pi
F32 = jnp.float32
BF16 = jnp.bfloat16

VMEM_SPEC = pl.BlockSpec(memory_space=pltpu.VMEM)
SMEM_SPEC = pl.BlockSpec(memory_space=pltpu.SMEM)


def padded_blocks(grid_width):
    return -(-(grid_width // BLOCK) // 16) * 16


def phase_rows(length, orders, blocks):
    digits = jnp.arange(RADIX, dtype=jnp.int32)
    steps = [digits, digits * RADIX, digits * RADIX * RADIX]
    steps.append(jnp.arange(blocks, dtype=jnp.int32) * BLOCK)
    steps = jnp.concatenate(steps)
    phases = steps[:, None] * orders[None, :] % length
    angles = phases.astype(F32) * (jnp.float32(FULL_TURN) / length.astype(F32))
    return jnp.cos(angles), jnp.sin(angles)


def table_kernel(cos_ref, sin_ref, active_ref, fc_ref, fs_ref, ca_ref, sa_ref):
    active = active_ref[...]
    cos_low = cos_ref[0:RADIX, :] * active
    sin_low = sin_ref[0:RADIX, :] * active
    cos_mid = cos_ref[RADIX : 2 * RADIX, :]
    sin_mid = sin_ref[RADIX : 2 * RADIX, :]
    for a in range(RADIX):
        c = cos_ref[2 * RADIX + a : 2 * RADIX + a + 1, :]
        s = sin_ref[2 * RADIX + a : 2 * RADIX + a + 1, :]
        ca_ref[a * RADIX : (a + 1) * RADIX, :] = c * cos_mid - s * sin_mid
        sa_ref[a * RADIX : (a + 1) * RADIX, :] = s * cos_mid + c * sin_mid

    def body(i, carry):
        cos_parts, sin_parts = [], []
        for k in range(2):
            c = ca_ref[pl.ds(2 * i + k, 1), :]
            s = sa_ref[pl.ds(2 * i + k, 1), :]
            cos_parts.append(c * cos_low - s * sin_low)
            sin_parts.append(-(s * cos_low + c * sin_low))
        rows = pl.ds(pl.multiple_of(i * 2 * RADIX, 2 * RADIX), 2 * RADIX)
        fc_ref[rows, :] = jnp.concatenate(cos_parts, axis=0).astype(BF16)
        fs_ref[rows, :] = jnp.concatenate(sin_parts, axis=0).astype(BF16)
        return carry

    lax.fori_loop(0, RADIX * RADIX // 2, body, 0)


def synthesize(coeffs, cos_block, sin_block, fc_ref, fs_ref, length, scale):
    fields = coeffs.shape[0] // 2
    blocks = cos_block.shape[0]
    reals, imags = [], []
    for v in range(fields):
        real = coeffs[2 * v : 2 * v + 1]
        imag = coeffs[2 * v + 1 : 2 * v + 2]
        reals.append((real * cos_block - imag * sin_block).astype(BF16))
        imags.append((real * sin_block + imag * cos_block).astype(BF16))
    dims = (((1,), (1,)), ((), ()))
    out = lax.dot_general(
        jnp.concatenate(reals, axis=0), fc_ref[...], dims, preferred_element_type=F32
    ) + lax.dot_general(
        jnp.concatenate(imags, axis=0), fs_ref[...], dims, preferred_element_type=F32
    )
    row = lax.broadcasted_iota(jnp.int32, out.shape, 0) % blocks
    point = row * BLOCK + lax.broadcasted_iota(jnp.int32, out.shape, 1)
    return jnp.where(point < length, out * scale, 0.0)


def synth_kernel(blocks, coef_ref, cos_ref, sin_ref, fc_ref, fs_ref, len_ref, scale_ref, out_ref):
    out_ref[...] = synthesize(
        coef_ref[...].astype(F32),
        cos_ref[3 * RADIX : 3 * RADIX + blocks, :],
        sin_ref[3 * RADIX : 3 * RADIX + blocks, :],
        fc_ref,
        fs_ref,
        len_ref[0],
        scale_ref[0],
    ).astype(BF16)


def gather_block(b, table, row_ref, col_ref, weight_ref, fields, blocks):
    stencil = col_ref.shape[0]
    half = 256
    lanes = pl.ds(pl.multiple_of(b * BLOCK, BLOCK), BLOCK)
    iota_half = lax.broadcasted_iota(jnp.int32, (half, BLOCK), 0).astype(F32).astype(BF16)
    iota_rows = lax.broadcasted_iota(jnp.int32, (3 * blocks, BLOCK), 0)
    one = jnp.ones((), BF16)
    zero = jnp.zeros((), BF16)
    acc = [jnp.zeros((blocks, BLOCK), F32) for _ in range(fields)]
    for p in range(stencil):
        col = col_ref[pl.ds(p, 1), lanes]
        row = row_ref[pl.ds(p, 1), lanes]
        weight = weight_ref[pl.ds(p, 1), lanes]
        point = col % BLOCK
        halves = []
        for h in range(BLOCK // half):
            local = point - h * half
            key = jnp.where((local >= 0) & (local < half), local, -1).astype(F32).astype(BF16)
            halves.append(jnp.where(iota_half == key, one, zero))
        onehot = jnp.concatenate(halves, axis=0)
        found = jnp.dot(table, onehot, preferred_element_type=F32)
        which = (row + 1) * blocks + col // BLOCK
        chosen = jnp.where(iota_rows == which, weight, 0.0)
        for r in range(3):
            sel = chosen[r * blocks : (r + 1) * blocks]
            for v in range(fields):
                start = (r * fields + v) * blocks
                acc[v] = acc[v] + found[start : start + blocks] * sel
    return [jnp.sum(a, axis=0, keepdims=True) for a in acc]


def advance(table_ref, row_ref, col_ref, weight_ref, new_ref, length, fields, blocks, real_blocks):
    new_ref[...] = jnp.zeros_like(new_ref)
    table = table_ref[...]

    def body(b, carry):
        interp = gather_block(b, table, row_ref, col_ref, weight_ref, fields, blocks)
        point = b * BLOCK + lax.broadcasted_iota(jnp.int32, (1, BLOCK), 1)
        for v in range(fields):
            value = interp[v] + 0.5 * interp[(v + 1) % fields] * jnp.tanh(interp[(v + 2) % fields])
            new_ref[pl.ds(v * blocks + b, 1), :] = jnp.where(point < length, value, 0.0)
        return carry

    lax.fori_loop(0, real_blocks, body, 0)


def analyse(new_ref, cos_block, sin_block, fc_ref, fs_ref, scale):
    blocks = cos_block.shape[0]
    fields = new_ref.shape[0] // blocks
    newgrid = new_ref[...].astype(BF16)
    part_real = jnp.dot(newgrid, fc_ref[...], preferred_element_type=F32)
    part_imag = jnp.dot(newgrid, fs_ref[...], preferred_element_type=F32)
    out = []
    for v in range(fields):
        pr = part_real[v * blocks : (v + 1) * blocks]
        pi = part_imag[v * blocks : (v + 1) * blocks]
        real = jnp.sum(pr * cos_block + pi * sin_block, axis=0, keepdims=True)
        imag = jnp.sum(pi * cos_block - pr * sin_block, axis=0, keepdims=True)
        out += [real * scale, imag * scale]
    return out


def grid_kernel(
    fields, blocks, real_blocks,
    table_ref, row_ref, col_ref, weight_ref, cos_ref, sin_ref, fc_ref, fs_ref, len_ref, scale_ref,
    out_ref, new_ref,
):
    advance(
        table_ref, row_ref, col_ref, weight_ref, new_ref, len_ref[0], fields, blocks, real_blocks
    )
    rows = analyse(
        new_ref,
        cos_ref[3 * RADIX : 3 * RADIX + blocks, :],
        sin_ref[3 * RADIX : 3 * RADIX + blocks, :],
        fc_ref,
        fs_ref,
        scale_ref[0],
    )
    out_ref[...] = jnp.concatenate(rows, axis=0).astype(BF16)


def per_device(
    spectrum,
    legendre,
    order_of_slot,
    reduced_length,
    gauss_weight,
    depart_row,
    depart_col,
    depart_weight,
):
    own_index = lax.axis_index("wave")
    count = lax.axis_size("wave")
    slot_count = legendre.shape[0]
    orders_total = order_of_slot.shape[0]
    variables, level_count = spectrum.shape[:2]
    assert level_count == 1
    steps = depart_row.shape[0]
    grid_width = depart_row.shape[-1]
    stencil = depart_row.shape[2]
    fields = variables
    real_blocks = grid_width // BLOCK
    blocks = padded_blocks(grid_width)

    own_orders = lax.dynamic_slice_in_dim(order_of_slot, own_index * slot_count, slot_count)
    degrees = jnp.arange(legendre.shape[2], dtype=jnp.int32)
    masked = jnp.where(
        degrees[None, None, :] >= own_orders[:, None, None], legendre, jnp.zeros((), BF16)
    )
    length = lax.dynamic_index_in_dim(reduced_length, own_index, keepdims=False)
    order_limit = jnp.minimum(orders_total, (length - 1) // 2)
    cos_rows, sin_rows = phase_rows(length, order_of_slot, blocks)
    active = (order_of_slot < order_limit).astype(F32)[None, :]
    fc, fs = pl.pallas_call(
        table_kernel,
        out_shape=[jax.ShapeDtypeStruct((BLOCK, orders_total), BF16)] * 2,
        in_specs=[VMEM_SPEC] * 3,
        out_specs=[VMEM_SPEC] * 2,
        scratch_shapes=[pltpu.VMEM((RADIX * RADIX, orders_total), F32)] * 2,
        name="table",
    )(cos_rows, sin_rows, active)
    length1 = length.reshape(1)
    grid_scale = (1.0 / jnp.sqrt(order_limit.astype(F32))).reshape(1)
    coef_scale = (gauss_weight[0] * jnp.sqrt(2.0 / length.astype(F32))).reshape(1)

    synth = pl.pallas_call(
        functools.partial(synth_kernel, blocks),
        out_shape=jax.ShapeDtypeStruct((fields * blocks, BLOCK), BF16),
        in_specs=[VMEM_SPEC] * 5 + [SMEM_SPEC] * 2,
        out_specs=VMEM_SPEC,
        name="synth",
    )
    grid_step = pl.pallas_call(
        functools.partial(grid_kernel, fields, blocks, real_blocks),
        out_shape=jax.ShapeDtypeStruct((2 * fields, orders_total), BF16),
        in_specs=[VMEM_SPEC] * 8 + [SMEM_SPEC] * 2,
        out_specs=VMEM_SPEC,
        scratch_shapes=[pltpu.VMEM((fields * blocks, BLOCK), F32)],
        name="grid_step",
    )
    spectral = spectrum.reshape(2 * fields, slot_count, -1)
    fourier = jnp.einsum("vsn,sjn->jvs", spectral, masked, preferred_element_type=F32)
    gram = jnp.einsum("sjn,skn->sjk", masked, masked, preferred_element_type=F32)
    forward = [(i, i + 1) for i in range(count - 1)]
    backward = [(i + 1, i) for i in range(count - 1)]
    for k in range(steps):
        gathered = lax.all_to_all(fourier.astype(BF16), "wave", split_axis=0, concat_axis=2, tiled=True)
        own = synth(
            gathered.reshape(2 * fields, orders_total), cos_rows, sin_rows, fc, fs, length1, grid_scale
        )
        low = lax.ppermute(own, "wave", forward)
        high = lax.ppermute(own, "wave", backward)
        coeffs = grid_step(
            jnp.concatenate([low, own, high], axis=0),
            depart_row[k].reshape(stencil, grid_width),
            depart_col[k].reshape(stencil, grid_width),
            depart_weight[k].reshape(stencil, grid_width),
            cos_rows, sin_rows, fc, fs, length1, coef_scale,
        )
        returned = lax.all_to_all(
            coeffs.reshape(1, 2 * fields, orders_total), "wave", split_axis=2, concat_axis=0, tiled=True
        )
        if k + 1 < steps:
            fourier = jnp.einsum("jvs,sjk->kvs", returned.astype(F32), gram, precision="highest")
    final = jnp.einsum("jvs,sjn->vsn", returned, masked, preferred_element_type=F32).astype(BF16)
    return final.reshape(spectrum.shape)


def solution(mesh):
    placed = (
        P(None, "lev", None, "wave", None),
        P("wave", None, None),
        P(),
        P(),
        P("wave"),
        P(None, "lev", None, "wave", None),
        P(None, "lev", None, "wave", None),
        P(None, "lev", None, "wave", None),
    )
    return jax.shard_map(
        per_device,
        mesh=mesh,
        in_specs=placed,
        out_specs=P(None, "lev", None, "wave", None),
        check_vma=False,
    )
```

```python
import functools
import math

import jax
import jax.numpy as jnp
from jax import lax
from jax.experimental import pallas as pl
from jax.experimental.pallas import tpu as pltpu
from jax.sharding import PartitionSpec as P

BLOCK = 512
RADIX = 8
FULL_TURN = 2.0 * math.pi
F32 = jnp.float32
BF16 = jnp.bfloat16

VMEM_SPEC = pl.BlockSpec(memory_space=pltpu.VMEM)
SMEM_SPEC = pl.BlockSpec(memory_space=pltpu.SMEM)


def padded_blocks(grid_width):
    return -(-(grid_width // BLOCK) // 16) * 16


def phase_rows(length, orders, blocks):
    digits = jnp.arange(RADIX, dtype=jnp.int32)
    steps = [digits, digits * RADIX, digits * RADIX * RADIX]
    steps.append(jnp.arange(blocks, dtype=jnp.int32) * BLOCK)
    steps = jnp.concatenate(steps)
    phases = steps[:, None] * orders[None, :] % length
    angles = phases.astype(F32) * (jnp.float32(FULL_TURN) / length.astype(F32))
    return jnp.cos(angles), jnp.sin(angles)


def build_table(cos_ref, sin_ref, active_ref, fc_ref, fs_ref, ca_ref, sa_ref):
    active = active_ref[...]
    cos_low = cos_ref[0:RADIX, :] * active
    sin_low = sin_ref[0:RADIX, :] * active
    cos_mid = cos_ref[RADIX : 2 * RADIX, :]
    sin_mid = sin_ref[RADIX : 2 * RADIX, :]
    for a in range(RADIX):
        c = cos_ref[2 * RADIX + a : 2 * RADIX + a + 1, :]
        s = sin_ref[2 * RADIX + a : 2 * RADIX + a + 1, :]
        ca_ref[a * RADIX : (a + 1) * RADIX, :] = c * cos_mid - s * sin_mid
        sa_ref[a * RADIX : (a + 1) * RADIX, :] = s * cos_mid + c * sin_mid

    def body(i, carry):
        cos_parts, sin_parts = [], []
        for k in range(2):
            c = ca_ref[pl.ds(2 * i + k, 1), :]
            s = sa_ref[pl.ds(2 * i + k, 1), :]
            cos_parts.append(c * cos_low - s * sin_low)
            sin_parts.append(-(s * cos_low + c * sin_low))
        rows = pl.ds(pl.multiple_of(i * 2 * RADIX, 2 * RADIX), 2 * RADIX)
        fc_ref[rows, :] = jnp.concatenate(cos_parts, axis=0).astype(BF16)
        fs_ref[rows, :] = jnp.concatenate(sin_parts, axis=0).astype(BF16)
        return carry

    lax.fori_loop(0, RADIX * RADIX // 2, body, 0)


def synthesize(coeffs, cos_block, sin_block, fc_ref, fs_ref, length, scale):
    fields = coeffs.shape[0] // 2
    blocks = cos_block.shape[0]
    reals, imags = [], []
    for v in range(fields):
        real = coeffs[2 * v : 2 * v + 1]
        imag = coeffs[2 * v + 1 : 2 * v + 2]
        reals.append((real * cos_block - imag * sin_block).astype(BF16))
        imags.append((real * sin_block + imag * cos_block).astype(BF16))
    dims = (((1,), (1,)), ((), ()))
    out = lax.dot_general(
        jnp.concatenate(reals, axis=0), fc_ref[...], dims, preferred_element_type=F32
    ) + lax.dot_general(
        jnp.concatenate(imags, axis=0), fs_ref[...], dims, preferred_element_type=F32
    )
    row = lax.broadcasted_iota(jnp.int32, out.shape, 0) % blocks
    point = row * BLOCK + lax.broadcasted_iota(jnp.int32, out.shape, 1)
    return jnp.where(point < length, out * scale, 0.0)


def synth_kernel(blocks, coef_ref, cos_ref, sin_ref, fc_ref, fs_ref, len_ref, scale_ref, out_ref):
    out_ref[...] = synthesize(
        coef_ref[...].astype(F32),
        cos_ref[3 * RADIX : 3 * RADIX + blocks, :],
        sin_ref[3 * RADIX : 3 * RADIX + blocks, :],
        fc_ref,
        fs_ref,
        len_ref[0],
        scale_ref[0],
    ).astype(BF16)


def gather_block(b, k, table, row_ref, col_ref, weight_ref, fields, blocks):
    stencil = col_ref.shape[1]
    half = 256
    lanes = pl.ds(pl.multiple_of(b * BLOCK, BLOCK), BLOCK)
    iota_half = lax.broadcasted_iota(jnp.int32, (half, BLOCK), 0).astype(F32).astype(BF16)
    iota_rows = lax.broadcasted_iota(jnp.int32, (3 * blocks, BLOCK), 0)
    one = jnp.ones((), BF16)
    zero = jnp.zeros((), BF16)
    acc = [jnp.zeros((blocks, BLOCK), F32) for _ in range(fields)]
    for p in range(stencil):
        col = col_ref[k, p, :, lanes]
        row = row_ref[k, p, :, lanes]
        weight = weight_ref[k, p, :, lanes]
        point = col % BLOCK
        halves = []
        for h in range(BLOCK // half):
            local = point - h * half
            key = jnp.where((local >= 0) & (local < half), local, -1).astype(F32).astype(BF16)
            halves.append(jnp.where(iota_half == key, one, zero))
        onehot = jnp.concatenate(halves, axis=0)
        found = jnp.dot(table, onehot, preferred_element_type=F32)
        which = (row + 1) * blocks + col // BLOCK
        chosen = jnp.where(iota_rows == which, weight, 0.0)
        for r in range(3):
            sel = chosen[r * blocks : (r + 1) * blocks]
            for v in range(fields):
                start = (r * fields + v) * blocks
                acc[v] = acc[v] + found[start : start + blocks] * sel
    return [jnp.sum(a, axis=0, keepdims=True) for a in acc]


def advance(table, k, row_ref, col_ref, weight_ref, new_ref, length, fields, blocks, real_blocks):
    new_ref[...] = jnp.zeros_like(new_ref)

    def body(b, carry):
        interp = gather_block(b, k, table, row_ref, col_ref, weight_ref, fields, blocks)
        point = b * BLOCK + lax.broadcasted_iota(jnp.int32, (1, BLOCK), 1)
        for v in range(fields):
            value = interp[v] + 0.5 * interp[(v + 1) % fields] * jnp.tanh(interp[(v + 2) % fields])
            new_ref[pl.ds(v * blocks + b, 1), :] = jnp.where(point < length, value, 0.0)
        return carry

    lax.fori_loop(0, real_blocks, body, 0)


def analyse(new_ref, cos_block, sin_block, fc_ref, fs_ref, scale):
    blocks = cos_block.shape[0]
    fields = new_ref.shape[0] // blocks
    newgrid = new_ref[...].astype(BF16)
    part_real = jnp.dot(newgrid, fc_ref[...], preferred_element_type=F32)
    part_imag = jnp.dot(newgrid, fs_ref[...], preferred_element_type=F32)
    out = []
    for v in range(fields):
        pr = part_real[v * blocks : (v + 1) * blocks]
        pi = part_imag[v * blocks : (v + 1) * blocks]
        real = jnp.sum(pr * cos_block + pi * sin_block, axis=0, keepdims=True)
        imag = jnp.sum(pi * cos_block - pr * sin_block, axis=0, keepdims=True)
        out += [real * scale, imag * scale]
    return out


def grid_kernel(
    fields, blocks, real_blocks,
    table_ref, row_ref, col_ref, weight_ref, cos_ref, sin_ref, fc_ref, fs_ref, len_ref, scale_ref,
    out_ref, new_ref,
):
    advance(
        table_ref[...], 0, row_ref, col_ref, weight_ref, new_ref, len_ref[0],
        fields, blocks, real_blocks,
    )
    rows = analyse(
        new_ref,
        cos_ref[3 * RADIX : 3 * RADIX + blocks, :],
        sin_ref[3 * RADIX : 3 * RADIX + blocks, :],
        fc_ref,
        fs_ref,
        scale_ref[0],
    )
    out_ref[...] = jnp.concatenate(rows, axis=0).astype(BF16)


GROUP = 16
MESH = pl.DeviceIdType.MESH


def forward_kernel(
    fields, slots, rows_j,
    orders_ref, spec_ref, leg_ref, send_ref, gram_ref, masked_ref, four_ref, gram_raw_ref, vjs_ref,
):
    g = pl.program_id(0)
    groups = pl.num_programs(0)
    first = lax.axis_index("wave") * slots + g * GROUP
    degree = lax.broadcasted_iota(jnp.int32, (rows_j, leg_ref.shape[1]), 1)
    for pair in range(GROUP // 2):
        parts = []
        for s in (2 * pair, 2 * pair + 1):
            rows = leg_ref[s * rows_j : (s + 1) * rows_j, :].astype(F32)
            parts.append(jnp.where(degree >= orders_ref[first + s], rows, 0.0))
        masked_ref[2 * pair * rows_j : 2 * (pair + 1) * rows_j, :] = jnp.concatenate(
            parts, axis=0
        ).astype(BF16)
    masked = masked_ref[...]
    state = spec_ref[...].reshape(fields * GROUP, spec_ref.shape[2])
    dims = (((1,), (1,)), ((), ()))
    size = GROUP * rows_j
    prod = lax.dot_general(masked, state, dims, preferred_element_type=F32)
    row = lax.broadcasted_iota(jnp.int32, (size, fields * GROUP), 0) // rows_j
    col = lax.broadcasted_iota(jnp.int32, (size, fields * GROUP), 1) % GROUP
    prod = jnp.where(row == col, prod, 0.0)
    four_ref[g] = jnp.sum(prod.reshape(GROUP, rows_j, fields * GROUP), axis=0)
    square = lax.dot_general(masked, masked, dims, preferred_element_type=F32)
    row = lax.broadcasted_iota(jnp.int32, (size, size), 0)
    col = lax.broadcasted_iota(jnp.int32, (size, size), 1)
    square = jnp.where(row // rows_j == col // rows_j, square, 0.0)
    diag = jnp.sum(square.reshape(GROUP, rows_j, size), axis=0)
    swap = (row // rows_j == col % GROUP) & (row % rows_j == col // GROUP)
    gram_raw_ref[g] = jnp.dot(
        diag, jnp.where(swap, 1.0, 0.0), preferred_element_type=F32, precision="highest"
    )

    @pl.when(g == groups - 1)
    def _():
        vjs_ref[...] = jnp.zeros_like(vjs_ref)
        gram_ref[...] = jnp.zeros_like(gram_ref)
        for h in range(slots // GROUP):
            lanes = slice(h * GROUP, (h + 1) * GROUP)
            for v in range(fields):
                vjs_ref[v, :, lanes] = four_ref[h, :, v * GROUP : (v + 1) * GROUP]
            for j in range(rows_j):
                gram_ref[j, :, lanes] = gram_raw_ref[h, :, j * GROUP : (j + 1) * GROUP]
        send_ref[...] = jnp.swapaxes(vjs_ref[...], 0, 1)


def inverse_kernel(fields, rows_j, coef_ref, masked_ref, out_ref):
    size = GROUP * rows_j
    row = lax.broadcasted_iota(jnp.int32, (size, fields * GROUP), 0) // rows_j
    col = lax.broadcasted_iota(jnp.int32, (size, fields * GROUP), 1) % GROUP
    tiled = jnp.concatenate([coef_ref[0]] * GROUP, axis=0)
    spread = jnp.where(row == col, tiled, 0.0).astype(BF16)
    out = lax.dot_general(
        spread, masked_ref[...], (((0,), (0,)), ((), ())), preferred_element_type=F32
    )
    out_ref[...] = out.astype(BF16).reshape(out_ref.shape)


def steps_kernel(
    steps, count, fields, blocks, real_blocks, slots,
    first_ref, gram_ref, cos_ref, sin_ref, active_ref, row_ref, col_ref, weight_ref,
    len_ref, grid_scale_ref, coef_scale_ref,
    out_ref,
    fc_ref, fs_ref, ca_ref, sa_ref, spec_send, spec_recv, grid_send, grid_recv, tab_ref, coef_ref,
    new_ref, spec_ssem, spec_rsem, grid_ssem, grid_rsem, halo_ssem, halo_rsem,
):
    tab_ref[...] = jnp.zeros_like(tab_ref)
    grid_send[...] = jnp.zeros_like(grid_send)
    me = lax.axis_index("wave")
    peers = [lax.rem(me + d, count) for d in range(1, count)]
    barrier = pltpu.get_barrier_semaphore()
    for peer in peers:
        pl.semaphore_signal(barrier, inc=1, device_id={"wave": peer}, device_id_type=MESH)
    pl.semaphore_wait(barrier, count - 1)

    def exchange(send, recv, ssem, rsem):
        copies = []
        for d, peer in enumerate(peers):
            copy = pltpu.make_async_remote_copy(
                src_ref=send.at[peer], dst_ref=recv.at[me], send_sem=ssem.at[d],
                recv_sem=rsem.at[d], device_id={"wave": peer}, device_id_type=MESH,
            )
            copy.start()
            copies.append(copy)
        return copies

    copies = exchange(first_ref, spec_recv.at[0], spec_ssem.at[0], spec_rsem.at[0])
    build_table(cos_ref, sin_ref, active_ref, fc_ref, fs_ref, ca_ref, sa_ref)
    cos_block = cos_ref[3 * RADIX : 3 * RADIX + blocks, :]
    sin_block = sin_ref[3 * RADIX : 3 * RADIX + blocks, :]
    rows = fields // 2 * blocks
    for k in range(steps):
        source = first_ref if k == 0 else spec_send.at[k - 1]
        for copy in copies:
            copy.wait()
        spec_recv[k, me] = source[me]
        for i in range(count):
            coef_ref[:, i * slots : (i + 1) * slots] = spec_recv[k, i, :, :slots]
        own = synthesize(
            coef_ref[...], cos_block, sin_block, fc_ref, fs_ref, len_ref[0], grid_scale_ref[0]
        )
        tab_ref[k, 1] = own.astype(BF16)
        up = pltpu.make_async_remote_copy(
            src_ref=tab_ref.at[k, 1], dst_ref=tab_ref.at[k, 0], send_sem=halo_ssem.at[k, 0],
            recv_sem=halo_rsem.at[k, 0], device_id={"wave": lax.rem(me + 1, count)},
            device_id_type=MESH,
        )
        down = pltpu.make_async_remote_copy(
            src_ref=tab_ref.at[k, 1], dst_ref=tab_ref.at[k, 2], send_sem=halo_ssem.at[k, 1],
            recv_sem=halo_rsem.at[k, 1], device_id={"wave": lax.rem(me + count - 1, count)},
            device_id_type=MESH,
        )

        @pl.when(me < count - 1)
        def _():
            up.start()

        @pl.when(me > 0)
        def _():
            down.start()
            up.wait_recv()

        @pl.when(me < count - 1)
        def _():
            down.wait_recv()

        table = tab_ref[k].reshape(3 * rows, BLOCK)
        advance(
            table, k, row_ref, col_ref, weight_ref, new_ref, len_ref[0],
            fields // 2, blocks, real_blocks,
        )

        @pl.when(me < count - 1)
        def _():
            up.wait_send()

        @pl.when(me > 0)
        def _():
            down.wait_send()

        parts = analyse(new_ref, cos_block, sin_block, fc_ref, fs_ref, coef_scale_ref[0])
        for v, part in enumerate(parts):
            coef_ref[v : v + 1, :] = part
        for i in range(count):
            grid_send[k, i, :, :slots] = coef_ref[:, i * slots : (i + 1) * slots]
        copies = exchange(grid_send.at[k], grid_recv.at[k], grid_ssem.at[k], grid_rsem.at[k])
        grid_recv[k, me] = grid_send[k, me]
        for copy in copies:
            copy.wait()
        if k + 1 < steps:
            mixed = []
            for v in range(fields):
                total = None
                for j in range(count):
                    term = gram_ref[j] * grid_recv[k, j, v : v + 1, :]
                    total = term if total is None else total + term
                mixed.append(total[None])
            spec_send[k] = jnp.swapaxes(jnp.concatenate(mixed, axis=0), 0, 1)
            copies = exchange(
                spec_send.at[k], spec_recv.at[k + 1], spec_ssem.at[k + 1], spec_rsem.at[k + 1]
            )
    last = jnp.swapaxes(grid_recv[steps - 1], 0, 1)
    for h in range(slots // GROUP):
        for v in range(fields):
            out_ref[h, :, v * GROUP : (v + 1) * GROUP] = last[v, :, h * GROUP : (h + 1) * GROUP]


def fused(spectrum, legendre, order_of_slot, length, gauss_weight, row, col, weight, count):
    slots, rows_j, degrees = legendre.shape
    fields = 2 * spectrum.shape[0]
    orders_total = order_of_slot.shape[0]
    steps, stencil, grid_width = row.shape[0], row.shape[2], row.shape[-1]
    real_blocks = grid_width // BLOCK
    blocks = padded_blocks(grid_width)
    groups = slots // GROUP
    size = GROUP * rows_j
    lanes = -(-slots // 128) * 128
    order_limit = jnp.minimum(orders_total, (length - 1) // 2)
    cos_rows, sin_rows = phase_rows(length, order_of_slot, blocks)
    active = (order_of_slot < order_limit).astype(F32)[None, :]
    grid_scale = (1.0 / jnp.sqrt(order_limit.astype(F32))).reshape(1)
    coef_scale = (gauss_weight[0] * jnp.sqrt(2.0 / length.astype(F32))).reshape(1)
    send, gram, masked = pl.pallas_call(
        functools.partial(forward_kernel, fields, slots, rows_j),
        grid=(groups,),
        out_shape=[
            jax.ShapeDtypeStruct((rows_j, fields, lanes), F32),
            jax.ShapeDtypeStruct((rows_j, rows_j, lanes), F32),
            jax.ShapeDtypeStruct((slots * rows_j, degrees), BF16),
        ],
        in_specs=[
            SMEM_SPEC,
            pl.BlockSpec((fields, GROUP, degrees), lambda g: (0, g, 0)),
            pl.BlockSpec((size, degrees), lambda g: (g, 0)),
        ],
        out_specs=[
            pl.BlockSpec((rows_j, fields, lanes), lambda g: (0, 0, 0)),
            pl.BlockSpec((rows_j, rows_j, lanes), lambda g: (0, 0, 0)),
            pl.BlockSpec((size, degrees), lambda g: (g, 0)),
        ],
        scratch_shapes=[
            pltpu.VMEM((groups, rows_j, fields * GROUP), F32),
            pltpu.VMEM((groups, rows_j, size), F32),
            pltpu.VMEM((fields, rows_j, lanes), F32),
        ],
        name="forward",
    )(order_of_slot, spectrum.reshape(fields, slots, degrees), legendre.reshape(slots * rows_j, degrees))
    shape = (steps, count, fields, lanes)
    table_rows = fields // 2 * blocks
    coeffs = pl.pallas_call(
        functools.partial(steps_kernel, steps, count, fields, blocks, real_blocks, slots),
        out_shape=jax.ShapeDtypeStruct((groups, rows_j, fields * GROUP), F32),
        in_specs=[VMEM_SPEC] * 8 + [SMEM_SPEC] * 3,
        out_specs=VMEM_SPEC,
        scratch_shapes=[pltpu.VMEM((BLOCK, orders_total), BF16)] * 2
        + [pltpu.VMEM((RADIX * RADIX, orders_total), F32)] * 2
        + [pltpu.VMEM(shape, F32)] * 4
        + [
            pltpu.VMEM((steps, 3, table_rows, BLOCK), BF16),
            pltpu.VMEM((fields, orders_total), F32),
            pltpu.VMEM((table_rows, BLOCK), F32),
        ]
        + [pltpu.SemaphoreType.DMA((steps, count - 1))] * 4
        + [pltpu.SemaphoreType.DMA((steps, 2))] * 2,
        compiler_params=pltpu.CompilerParams(collective_id=0, has_side_effects=True),
        name="steps",
    )(
        send, gram, cos_rows, sin_rows, active,
        row.reshape(steps, stencil, 1, grid_width),
        col.reshape(steps, stencil, 1, grid_width),
        weight.reshape(steps, stencil, 1, grid_width),
        length.reshape(1), grid_scale, coef_scale,
    )
    out = pl.pallas_call(
        functools.partial(inverse_kernel, fields, rows_j),
        grid=(groups,),
        out_shape=jax.ShapeDtypeStruct((fields, slots, degrees), BF16),
        in_specs=[
            pl.BlockSpec((1, rows_j, fields * GROUP), lambda g: (g, 0, 0)),
            pl.BlockSpec((size, degrees), lambda g: (g, 0)),
        ],
        out_specs=pl.BlockSpec((fields, GROUP, degrees), lambda g: (0, g, 0)),
        name="inverse",
    )(coeffs, masked)
    return out.reshape(spectrum.shape)


def per_device(
    spectrum,
    legendre,
    order_of_slot,
    reduced_length,
    gauss_weight,
    depart_row,
    depart_col,
    depart_weight,
):
    own_index = lax.axis_index("wave")
    count = lax.axis_size("wave")
    slot_count = legendre.shape[0]
    orders_total = order_of_slot.shape[0]
    variables, level_count = spectrum.shape[:2]
    assert level_count == 1
    steps = depart_row.shape[0]
    grid_width = depart_row.shape[-1]
    stencil = depart_row.shape[2]
    fields = variables
    real_blocks = grid_width // BLOCK
    blocks = padded_blocks(grid_width)

    length = lax.dynamic_index_in_dim(reduced_length, own_index, keepdims=False)
    fits = slot_count % GROUP == 0 and 2 * fields == 8
    if fits and legendre.shape[1] == 8 and count == 8:
        return fused(
            spectrum, legendre, order_of_slot, length, gauss_weight,
            depart_row, depart_col, depart_weight, count,
        )

    own_orders = lax.dynamic_slice_in_dim(order_of_slot, own_index * slot_count, slot_count)
    degrees = jnp.arange(legendre.shape[2], dtype=jnp.int32)
    masked = jnp.where(
        degrees[None, None, :] >= own_orders[:, None, None], legendre, jnp.zeros((), BF16)
    )
    order_limit = jnp.minimum(orders_total, (length - 1) // 2)
    cos_rows, sin_rows = phase_rows(length, order_of_slot, blocks)
    active = (order_of_slot < order_limit).astype(F32)[None, :]
    fc, fs = pl.pallas_call(
        build_table,
        out_shape=[jax.ShapeDtypeStruct((BLOCK, orders_total), BF16)] * 2,
        in_specs=[VMEM_SPEC] * 3,
        out_specs=[VMEM_SPEC] * 2,
        scratch_shapes=[pltpu.VMEM((RADIX * RADIX, orders_total), F32)] * 2,
        name="table",
    )(cos_rows, sin_rows, active)
    length1 = length.reshape(1)
    grid_scale = (1.0 / jnp.sqrt(order_limit.astype(F32))).reshape(1)
    coef_scale = (gauss_weight[0] * jnp.sqrt(2.0 / length.astype(F32))).reshape(1)

    synth = pl.pallas_call(
        functools.partial(synth_kernel, blocks),
        out_shape=jax.ShapeDtypeStruct((fields * blocks, BLOCK), BF16),
        in_specs=[VMEM_SPEC] * 5 + [SMEM_SPEC] * 2,
        out_specs=VMEM_SPEC,
        name="synth",
    )
    grid_step = pl.pallas_call(
        functools.partial(grid_kernel, fields, blocks, real_blocks),
        out_shape=jax.ShapeDtypeStruct((2 * fields, orders_total), BF16),
        in_specs=[VMEM_SPEC] * 8 + [SMEM_SPEC] * 2,
        out_specs=VMEM_SPEC,
        scratch_shapes=[pltpu.VMEM((fields * blocks, BLOCK), F32)],
        name="grid_step",
    )
    spectral = spectrum.reshape(2 * fields, slot_count, -1)
    fourier = jnp.einsum("vsn,sjn->jvs", spectral, masked, preferred_element_type=F32)
    gram = jnp.einsum("sjn,skn->sjk", masked, masked, preferred_element_type=F32)
    forward = [(i, i + 1) for i in range(count - 1)]
    backward = [(i + 1, i) for i in range(count - 1)]
    for k in range(steps):
        gathered = lax.all_to_all(fourier.astype(BF16), "wave", split_axis=0, concat_axis=2, tiled=True)
        own = synth(
            gathered.reshape(2 * fields, orders_total), cos_rows, sin_rows, fc, fs, length1, grid_scale
        )
        low = lax.ppermute(own, "wave", forward)
        high = lax.ppermute(own, "wave", backward)
        coeffs = grid_step(
            jnp.concatenate([low, own, high], axis=0),
            depart_row[k].reshape(1, stencil, 1, grid_width),
            depart_col[k].reshape(1, stencil, 1, grid_width),
            depart_weight[k].reshape(1, stencil, 1, grid_width),
            cos_rows, sin_rows, fc, fs, length1, coef_scale,
        )
        returned = lax.all_to_all(
            coeffs.reshape(1, 2 * fields, orders_total), "wave", split_axis=2, concat_axis=0, tiled=True
        )
        if k + 1 < steps:
            fourier = jnp.einsum("jvs,sjk->kvs", returned.astype(F32), gram, precision="highest")
    final = jnp.einsum("jvs,sjn->vsn", returned, masked, preferred_element_type=F32).astype(BF16)
    return final.reshape(spectrum.shape)


def solution(mesh):
    placed = (
        P(None, "lev", None, "wave", None),
        P("wave", None, None),
        P(),
        P(),
        P("wave"),
        P(None, "lev", None, "wave", None),
        P(None, "lev", None, "wave", None),
        P(None, "lev", None, "wave", None),
    )
    return jax.shard_map(
        per_device,
        mesh=mesh,
        in_specs=placed,
        out_specs=P(None, "lev", None, "wave", None),
        check_vma=False,
    )
```

```python
import functools
import math

import jax
import jax.numpy as jnp
from jax import lax
from jax.experimental import pallas as pl
from jax.experimental.pallas import tpu as pltpu
from jax.sharding import PartitionSpec as P

BLOCK = 512
RADIX = 8
FULL_TURN = 2.0 * math.pi
F32 = jnp.float32
BF16 = jnp.bfloat16

VMEM_SPEC = pl.BlockSpec(memory_space=pltpu.VMEM)
SMEM_SPEC = pl.BlockSpec(memory_space=pltpu.SMEM)


def padded_blocks(grid_width):
    return -(-(grid_width // BLOCK) // 16) * 16


def phase_rows(length, orders, blocks):
    digits = jnp.arange(RADIX, dtype=jnp.int32)
    steps = [digits, digits * RADIX, digits * RADIX * RADIX]
    steps.append(jnp.arange(blocks, dtype=jnp.int32) * BLOCK)
    steps = jnp.concatenate(steps)
    phases = steps[:, None] * orders[None, :] % length
    angles = phases.astype(F32) * (jnp.float32(FULL_TURN) / length.astype(F32))
    return jnp.cos(angles), jnp.sin(angles)


def build_table(cos_ref, sin_ref, active_ref, fc_ref, fs_ref, ca_ref, sa_ref):
    active = active_ref[...]
    cos_low = cos_ref[0:RADIX, :] * active
    sin_low = sin_ref[0:RADIX, :] * active
    cos_mid = cos_ref[RADIX : 2 * RADIX, :]
    sin_mid = sin_ref[RADIX : 2 * RADIX, :]
    for a in range(RADIX):
        c = cos_ref[2 * RADIX + a : 2 * RADIX + a + 1, :]
        s = sin_ref[2 * RADIX + a : 2 * RADIX + a + 1, :]
        ca_ref[a * RADIX : (a + 1) * RADIX, :] = c * cos_mid - s * sin_mid
        sa_ref[a * RADIX : (a + 1) * RADIX, :] = s * cos_mid + c * sin_mid

    def body(i, carry):
        cos_parts, sin_parts = [], []
        for k in range(2):
            c = ca_ref[pl.ds(2 * i + k, 1), :]
            s = sa_ref[pl.ds(2 * i + k, 1), :]
            cos_parts.append(c * cos_low - s * sin_low)
            sin_parts.append(-(s * cos_low + c * sin_low))
        rows = pl.ds(pl.multiple_of(i * 2 * RADIX, 2 * RADIX), 2 * RADIX)
        fc_ref[rows, :] = jnp.concatenate(cos_parts, axis=0).astype(BF16)
        fs_ref[rows, :] = jnp.concatenate(sin_parts, axis=0).astype(BF16)
        return carry

    lax.fori_loop(0, RADIX * RADIX // 2, body, 0)


def synthesize(coeffs, cos_block, sin_block, fc_ref, fs_ref, length, scale):
    fields = coeffs.shape[0] // 2
    blocks = cos_block.shape[0]
    reals, imags = [], []
    for v in range(fields):
        real = coeffs[2 * v : 2 * v + 1]
        imag = coeffs[2 * v + 1 : 2 * v + 2]
        reals.append((real * cos_block - imag * sin_block).astype(BF16))
        imags.append((real * sin_block + imag * cos_block).astype(BF16))
    dims = (((1,), (1,)), ((), ()))
    out = lax.dot_general(
        jnp.concatenate(reals, axis=0), fc_ref[...], dims, preferred_element_type=F32
    ) + lax.dot_general(
        jnp.concatenate(imags, axis=0), fs_ref[...], dims, preferred_element_type=F32
    )
    row = lax.broadcasted_iota(jnp.int32, out.shape, 0) % blocks
    point = row * BLOCK + lax.broadcasted_iota(jnp.int32, out.shape, 1)
    return jnp.where(point < length, out * scale, 0.0)


def synth_kernel(blocks, coef_ref, cos_ref, sin_ref, fc_ref, fs_ref, len_ref, scale_ref, out_ref):
    out_ref[...] = synthesize(
        coef_ref[...].astype(F32),
        cos_ref[3 * RADIX : 3 * RADIX + blocks, :],
        sin_ref[3 * RADIX : 3 * RADIX + blocks, :],
        fc_ref,
        fs_ref,
        len_ref[0],
        scale_ref[0],
    ).astype(BF16)


def gather_block(b, k, table, row_ref, col_ref, weight_ref, fields, blocks):
    stencil = col_ref.shape[1]
    half = 256
    lanes = pl.ds(pl.multiple_of(b * BLOCK, BLOCK), BLOCK)
    iota_half = lax.broadcasted_iota(jnp.int32, (half, BLOCK), 0).astype(F32).astype(BF16)
    iota_rows = lax.broadcasted_iota(jnp.int32, (3 * blocks, BLOCK), 0)
    one = jnp.ones((), BF16)
    zero = jnp.zeros((), BF16)
    acc = [jnp.zeros((blocks, BLOCK), F32) for _ in range(fields)]
    for p in range(stencil):
        col = col_ref[k, p, :, lanes]
        row = row_ref[k, p, :, lanes]
        weight = weight_ref[k, p, :, lanes]
        point = col % BLOCK
        halves = []
        for h in range(BLOCK // half):
            local = point - h * half
            key = jnp.where((local >= 0) & (local < half), local, -1).astype(F32).astype(BF16)
            halves.append(jnp.where(iota_half == key, one, zero))
        onehot = jnp.concatenate(halves, axis=0)
        found = jnp.dot(table, onehot, preferred_element_type=F32)
        which = (row + 1) * blocks + col // BLOCK
        chosen = jnp.where(iota_rows == which, weight, 0.0)
        for r in range(3):
            sel = chosen[r * blocks : (r + 1) * blocks]
            for v in range(fields):
                start = (r * fields + v) * blocks
                acc[v] = acc[v] + found[start : start + blocks] * sel
    return [jnp.sum(a, axis=0, keepdims=True) for a in acc]


def advance(table, k, row_ref, col_ref, weight_ref, new_ref, length, fields, blocks, real_blocks):
    new_ref[...] = jnp.zeros_like(new_ref)

    def body(b, carry):
        interp = gather_block(b, k, table, row_ref, col_ref, weight_ref, fields, blocks)
        point = b * BLOCK + lax.broadcasted_iota(jnp.int32, (1, BLOCK), 1)
        for v in range(fields):
            value = interp[v] + 0.5 * interp[(v + 1) % fields] * jnp.tanh(interp[(v + 2) % fields])
            new_ref[pl.ds(v * blocks + b, 1), :] = jnp.where(point < length, value, 0.0)
        return carry

    lax.fori_loop(0, real_blocks, body, 0)


def analyse(new_ref, cos_block, sin_block, fc_ref, fs_ref, scale):
    blocks = cos_block.shape[0]
    fields = new_ref.shape[0] // blocks
    newgrid = new_ref[...].astype(BF16)
    part_real = jnp.dot(newgrid, fc_ref[...], preferred_element_type=F32)
    part_imag = jnp.dot(newgrid, fs_ref[...], preferred_element_type=F32)
    out = []
    for v in range(fields):
        pr = part_real[v * blocks : (v + 1) * blocks]
        pi = part_imag[v * blocks : (v + 1) * blocks]
        real = jnp.sum(pr * cos_block + pi * sin_block, axis=0, keepdims=True)
        imag = jnp.sum(pi * cos_block - pr * sin_block, axis=0, keepdims=True)
        out += [real * scale, imag * scale]
    return out


def grid_kernel(
    fields, blocks, real_blocks,
    table_ref, row_ref, col_ref, weight_ref, cos_ref, sin_ref, fc_ref, fs_ref, len_ref, scale_ref,
    out_ref, new_ref,
):
    advance(
        table_ref[...], 0, row_ref, col_ref, weight_ref, new_ref, len_ref[0],
        fields, blocks, real_blocks,
    )
    rows = analyse(
        new_ref,
        cos_ref[3 * RADIX : 3 * RADIX + blocks, :],
        sin_ref[3 * RADIX : 3 * RADIX + blocks, :],
        fc_ref,
        fs_ref,
        scale_ref[0],
    )
    out_ref[...] = jnp.concatenate(rows, axis=0).astype(BF16)


HALF = 256


def fill_phases(orders, length, cos_ref, sin_ref):
    limit = length.astype(F32)
    inverse = 1.0 / jnp.full(orders.shape, limit)
    turn = FULL_TURN / jnp.full(orders.shape, limit)
    digit = lax.broadcasted_iota(jnp.int32, (RADIX, orders.shape[1]), 0)
    for t in range(cos_ref.shape[0] // RADIX):
        if t < 3:
            step = digit * RADIX**t
        else:
            step = (digit + (t - 3) * RADIX) * BLOCK
        product = step * orders
        rest = product - jnp.floor(product.astype(F32) * inverse).astype(jnp.int32) * length
        rest = jnp.where(rest < 0, rest + length, rest)
        rest = jnp.where(rest >= length, rest - length, rest)
        angle = rest.astype(F32) * turn
        cos_ref[t * RADIX : (t + 1) * RADIX, :] = jnp.cos(angle)
        sin_ref[t * RADIX : (t + 1) * RADIX, :] = jnp.sin(angle)


def grid_rows(coeffs, cos_block, sin_block, fc_ref, fs_ref, length, scale):
    fields = coeffs.shape[0] // 2
    blocks = cos_block.shape[0]
    reals, imags = [], []
    for v in range(fields):
        real = coeffs[2 * v : 2 * v + 1]
        imag = coeffs[2 * v + 1 : 2 * v + 2]
        reals.append((real * cos_block - imag * sin_block).astype(BF16))
        imags.append((real * sin_block + imag * cos_block).astype(BF16))
    dims = (((1,), (1,)), ((), ()))
    out = lax.dot_general(
        fc_ref[...], jnp.concatenate(reals, axis=0), dims, preferred_element_type=F32
    ) + lax.dot_general(
        fs_ref[...], jnp.concatenate(imags, axis=0), dims, preferred_element_type=F32
    )
    out = out.T
    row = lax.broadcasted_iota(jnp.int32, out.shape, 0) % blocks
    point = row * BLOCK + lax.broadcasted_iota(jnp.int32, out.shape, 1)
    out = jnp.where(point < length, out * scale, 0.0)
    parts = []
    for v in range(fields):
        rows = out[v * blocks : (v + 1) * blocks]
        parts += [rows[:8, :HALF], rows[:8, HALF:], rows[8:12, :HALF], rows[8:12, HALF:]]
    return jnp.concatenate(parts, axis=0)


def pick_block(b, k, table, row_ref, col_ref, weight_ref, fields):
    stencil = col_ref.shape[1]
    lanes = pl.ds(pl.multiple_of(b * BLOCK, BLOCK), BLOCK)
    iota = lax.broadcasted_iota(jnp.int32, (HALF, BLOCK), 0).astype(F32).astype(BF16)
    sub = lax.broadcasted_iota(jnp.int32, (8, BLOCK), 0)
    one = jnp.ones((), BF16)
    zero = jnp.zeros((), BF16)
    acc = [jnp.zeros((8, BLOCK), F32) for _ in range(fields)]
    for p in range(stencil):
        col = col_ref[k, p, :, lanes]
        row = row_ref[k, p, :, lanes]
        weight = weight_ref[k, p, :, lanes]
        key = (col & (HALF - 1)).astype(F32).astype(BF16)
        onehot = jnp.where(iota == key, one, zero)
        found = jnp.dot(table, onehot, preferred_element_type=F32)
        big = col // BLOCK
        side = (col // HALF) & 1
        which = (row + 1) * 24 + jnp.where(big < 8, side * 8 + big, 8 + side * 4 + big)
        got = [jnp.zeros((8, BLOCK), F32) for _ in range(fields)]
        for r in range(3):
            for t in range(3):
                hit = sub == which - (r * 24 + t * 8)
                for v in range(fields):
                    start = (r * fields + v) * 24 + t * 8
                    got[v] = jnp.where(hit, found[start : start + 8], got[v])
        for v in range(fields):
            acc[v] = acc[v] + got[v] * weight
    return [jnp.sum(a, axis=0, keepdims=True) for a in acc]


def advance_fast(table, k, row_ref, col_ref, weight_ref, new_ref, length, fields, blocks, real_blocks):
    new_ref[...] = jnp.zeros_like(new_ref)

    def body(b, carry):
        interp = pick_block(b, k, table, row_ref, col_ref, weight_ref, fields)
        point = b * BLOCK + lax.broadcasted_iota(jnp.int32, (1, BLOCK), 1)
        for v in range(fields):
            value = interp[v] + 0.5 * interp[(v + 1) % fields] * jnp.tanh(interp[(v + 2) % fields])
            new_ref[pl.ds(v * blocks + b, 1), :] = jnp.where(point < length, value, 0.0)
        return carry

    lax.fori_loop(0, real_blocks, body, 0)


GROUP = 16
MESH = pl.DeviceIdType.MESH


def forward_kernel(
    fields, slots, rows_j,
    orders_ref, spec_ref, leg_ref, send_ref, gram_ref, masked_ref, four_ref, gram_raw_ref, vjs_ref,
):
    g = pl.program_id(0)
    groups = pl.num_programs(0)
    first = lax.axis_index("wave") * slots + g * GROUP
    degree = lax.broadcasted_iota(jnp.int32, (rows_j, leg_ref.shape[1]), 1)
    for pair in range(GROUP // 2):
        parts = []
        for s in (2 * pair, 2 * pair + 1):
            rows = leg_ref[s * rows_j : (s + 1) * rows_j, :].astype(F32)
            parts.append(jnp.where(degree >= orders_ref[first + s], rows, 0.0))
        masked_ref[2 * pair * rows_j : 2 * (pair + 1) * rows_j, :] = jnp.concatenate(
            parts, axis=0
        ).astype(BF16)
    masked = masked_ref[...]
    state = spec_ref[...].reshape(fields * GROUP, spec_ref.shape[2])
    dims = (((1,), (1,)), ((), ()))
    size = GROUP * rows_j
    both = lax.dot_general(
        masked, jnp.concatenate([state, masked], axis=0), dims, preferred_element_type=F32
    )
    prod = both[:, : fields * GROUP]
    row = lax.broadcasted_iota(jnp.int32, (size, fields * GROUP), 0) // rows_j
    col = lax.broadcasted_iota(jnp.int32, (size, fields * GROUP), 1) % GROUP
    prod = jnp.where(row == col, prod, 0.0)
    four_ref[g] = jnp.sum(prod.reshape(GROUP, rows_j, fields * GROUP), axis=0)
    square = both[:, fields * GROUP :]
    row = lax.broadcasted_iota(jnp.int32, (size, size), 0)
    col = lax.broadcasted_iota(jnp.int32, (size, size), 1)
    square = jnp.where(row // rows_j == col // rows_j, square, 0.0)
    diag = jnp.sum(square.reshape(GROUP, rows_j, size), axis=0)
    swap = (row // rows_j == col % GROUP) & (row % rows_j == col // GROUP)
    gram_raw_ref[g] = jnp.dot(
        diag, jnp.where(swap, 1.0, 0.0), preferred_element_type=F32, precision="highest"
    )

    @pl.when(g == groups - 1)
    def _():
        vjs_ref[...] = jnp.zeros_like(vjs_ref)
        gram_ref[...] = jnp.zeros_like(gram_ref)
        for h in range(slots // GROUP):
            lanes = slice(h * GROUP, (h + 1) * GROUP)
            for v in range(fields):
                vjs_ref[v, :, lanes] = four_ref[h, :, v * GROUP : (v + 1) * GROUP]
            for j in range(rows_j):
                gram_ref[j, :, lanes] = gram_raw_ref[h, :, j * GROUP : (j + 1) * GROUP]
        send_ref[...] = jnp.swapaxes(vjs_ref[...], 0, 1)


def inverse_kernel(fields, rows_j, coef_ref, masked_ref, out_ref):
    size = GROUP * rows_j
    row = lax.broadcasted_iota(jnp.int32, (size, fields * GROUP), 0) // rows_j
    col = lax.broadcasted_iota(jnp.int32, (size, fields * GROUP), 1) % GROUP
    tiled = jnp.concatenate([coef_ref[0]] * GROUP, axis=0)
    spread = jnp.where(row == col, tiled, 0.0).astype(BF16)
    out = lax.dot_general(
        spread, masked_ref[...], (((0,), (0,)), ((), ())), preferred_element_type=F32
    )
    out_ref[...] = out.astype(BF16).reshape(out_ref.shape)


def steps_kernel(
    steps, count, fields, blocks, real_blocks, slots,
    first_ref, gram_ref, orders_ref, row_ref, col_ref, weight_ref, len_ref, gauss_ref,
    out_ref,
    cos_ref, sin_ref, fc_ref, fs_ref, ca_ref, sa_ref, spec_send, spec_recv, grid_send, grid_recv, tab_ref, coef_ref,
    new_ref, spec_ssem, spec_rsem, grid_ssem, grid_rsem, halo_ssem, halo_rsem,
):
    tab_ref[...] = jnp.zeros_like(tab_ref)
    grid_send[...] = jnp.zeros_like(grid_send)
    me = lax.axis_index("wave")
    peers = [lax.rem(me + d, count) for d in range(1, count)]
    barrier = pltpu.get_barrier_semaphore()
    for peer in peers:
        pl.semaphore_signal(barrier, inc=1, device_id={"wave": peer}, device_id_type=MESH)
    pl.semaphore_wait(barrier, count - 1)

    def exchange(send, recv, ssem, rsem):
        copies = []
        for d, peer in enumerate(peers):
            copy = pltpu.make_async_remote_copy(
                src_ref=send.at[peer], dst_ref=recv.at[me], send_sem=ssem.at[d],
                recv_sem=rsem.at[d], device_id={"wave": peer}, device_id_type=MESH,
            )
            copy.start()
            copies.append(copy)
        return copies

    copies = exchange(first_ref, spec_recv.at[0], spec_ssem.at[0], spec_rsem.at[0])
    length = len_ref[me]
    orders = orders_ref[...]
    limit = jnp.minimum(orders.shape[1], (length - 1) // 2)
    fill_phases(orders, length, cos_ref, sin_ref)
    active = jnp.where(orders < limit, 1.0, 0.0)
    build_table(cos_ref, sin_ref, active, fc_ref, fs_ref, ca_ref, sa_ref)
    grid_scale = 1.0 / jnp.sqrt(jnp.full((1, BLOCK), limit.astype(F32)))
    coef_scale = gauss_ref[0] * jnp.sqrt(2.0 / jnp.full(orders.shape, length.astype(F32)))
    cos_block = cos_ref[3 * RADIX : 3 * RADIX + blocks, :]
    sin_block = sin_ref[3 * RADIX : 3 * RADIX + blocks, :]
    rows = fields // 2 * 24
    for k in range(steps):
        source = first_ref if k == 0 else spec_send.at[k - 1]
        for copy in copies:
            copy.wait()
        spec_recv[k, me] = source[me]
        for i in range(count):
            coef_ref[:, i * slots : (i + 1) * slots] = spec_recv[k, i, :, :slots]
        own = grid_rows(
            coef_ref[...], cos_block, sin_block, fc_ref, fs_ref, length, grid_scale
        )
        tab_ref[k, 1] = own.astype(BF16)
        up = pltpu.make_async_remote_copy(
            src_ref=tab_ref.at[k, 1], dst_ref=tab_ref.at[k, 0], send_sem=halo_ssem.at[k, 0],
            recv_sem=halo_rsem.at[k, 0], device_id={"wave": lax.rem(me + 1, count)},
            device_id_type=MESH,
        )
        down = pltpu.make_async_remote_copy(
            src_ref=tab_ref.at[k, 1], dst_ref=tab_ref.at[k, 2], send_sem=halo_ssem.at[k, 1],
            recv_sem=halo_rsem.at[k, 1], device_id={"wave": lax.rem(me + count - 1, count)},
            device_id_type=MESH,
        )

        @pl.when(me < count - 1)
        def _():
            up.start()

        @pl.when(me > 0)
        def _():
            down.start()
            up.wait_recv()

        @pl.when(me < count - 1)
        def _():
            down.wait_recv()

        table = tab_ref[k].reshape(3 * rows, HALF)
        advance_fast(
            table, k, row_ref, col_ref, weight_ref, new_ref, length,
            fields // 2, blocks, real_blocks,
        )

        @pl.when(me < count - 1)
        def _():
            up.wait_send()

        @pl.when(me > 0)
        def _():
            down.wait_send()

        parts = analyse(new_ref, cos_block, sin_block, fc_ref, fs_ref, coef_scale)
        for v, part in enumerate(parts):
            coef_ref[v : v + 1, :] = part
        for i in range(count):
            grid_send[k, i, :, :slots] = coef_ref[:, i * slots : (i + 1) * slots]
        copies = exchange(grid_send.at[k], grid_recv.at[k], grid_ssem.at[k], grid_rsem.at[k])
        grid_recv[k, me] = grid_send[k, me]
        for copy in copies:
            copy.wait()
        if k + 1 < steps:
            mixed = []
            for v in range(fields):
                total = None
                for j in range(count):
                    term = gram_ref[j] * grid_recv[k, j, v : v + 1, :]
                    total = term if total is None else total + term
                mixed.append(total[None])
            spec_send[k] = jnp.swapaxes(jnp.concatenate(mixed, axis=0), 0, 1)
            copies = exchange(
                spec_send.at[k], spec_recv.at[k + 1], spec_ssem.at[k + 1], spec_rsem.at[k + 1]
            )
    last = jnp.swapaxes(grid_recv[steps - 1], 0, 1)
    for h in range(slots // GROUP):
        for v in range(fields):
            out_ref[h, :, v * GROUP : (v + 1) * GROUP] = last[v, :, h * GROUP : (h + 1) * GROUP]


def fused(spectrum, legendre, order_of_slot, reduced_length, gauss_weight, row, col, weight, count):
    slots, rows_j, degrees = legendre.shape
    fields = 2 * spectrum.shape[0]
    orders_total = order_of_slot.shape[0]
    steps, stencil, grid_width = row.shape[0], row.shape[2], row.shape[-1]
    real_blocks = grid_width // BLOCK
    blocks = padded_blocks(grid_width)
    groups = slots // GROUP
    size = GROUP * rows_j
    lanes = -(-slots // 128) * 128
    send, gram, masked = pl.pallas_call(
        functools.partial(forward_kernel, fields, slots, rows_j),
        grid=(groups,),
        out_shape=[
            jax.ShapeDtypeStruct((rows_j, fields, lanes), F32),
            jax.ShapeDtypeStruct((rows_j, rows_j, lanes), F32),
            jax.ShapeDtypeStruct((slots * rows_j, degrees), BF16),
        ],
        in_specs=[
            SMEM_SPEC,
            pl.BlockSpec((fields, GROUP, degrees), lambda g: (0, g, 0)),
            pl.BlockSpec((size, degrees), lambda g: (g, 0)),
        ],
        out_specs=[
            pl.BlockSpec((rows_j, fields, lanes), lambda g: (0, 0, 0)),
            pl.BlockSpec((rows_j, rows_j, lanes), lambda g: (0, 0, 0)),
            pl.BlockSpec((size, degrees), lambda g: (g, 0)),
        ],
        scratch_shapes=[
            pltpu.VMEM((groups, rows_j, fields * GROUP), F32),
            pltpu.VMEM((groups, rows_j, size), F32),
            pltpu.VMEM((fields, rows_j, lanes), F32),
        ],
        name="forward",
    )(order_of_slot, spectrum.reshape(fields, slots, degrees), legendre.reshape(slots * rows_j, degrees))
    shape = (steps, count, fields, lanes)
    table_rows = fields // 2 * blocks
    coeffs = pl.pallas_call(
        functools.partial(steps_kernel, steps, count, fields, blocks, real_blocks, slots),
        out_shape=jax.ShapeDtypeStruct((groups, rows_j, fields * GROUP), F32),
        in_specs=[VMEM_SPEC] * 6 + [SMEM_SPEC] * 2,
        out_specs=VMEM_SPEC,
        scratch_shapes=[pltpu.VMEM((3 * RADIX + blocks, orders_total), F32)] * 2
        + [pltpu.VMEM((BLOCK, orders_total), BF16)] * 2
        + [pltpu.VMEM((RADIX * RADIX, orders_total), F32)] * 2
        + [pltpu.VMEM(shape, F32)] * 4
        + [
            pltpu.VMEM((steps, 3, fields // 2 * 24, HALF), BF16),
            pltpu.VMEM((fields, orders_total), F32),
            pltpu.VMEM((table_rows, BLOCK), F32),
        ]
        + [pltpu.SemaphoreType.DMA((steps, count - 1))] * 4
        + [pltpu.SemaphoreType.DMA((steps, 2))] * 2,
        compiler_params=pltpu.CompilerParams(collective_id=0, has_side_effects=True),
        name="steps",
    )(
        send, gram, order_of_slot.reshape(1, orders_total),
        row.reshape(steps, stencil, 1, grid_width),
        col.reshape(steps, stencil, 1, grid_width),
        weight.reshape(steps, stencil, 1, grid_width),
        reduced_length, gauss_weight,
    )
    out = pl.pallas_call(
        functools.partial(inverse_kernel, fields, rows_j),
        grid=(groups,),
        out_shape=jax.ShapeDtypeStruct((fields, slots, degrees), BF16),
        in_specs=[
            pl.BlockSpec((1, rows_j, fields * GROUP), lambda g: (g, 0, 0)),
            pl.BlockSpec((size, degrees), lambda g: (g, 0)),
        ],
        out_specs=pl.BlockSpec((fields, GROUP, degrees), lambda g: (0, g, 0)),
        name="inverse",
    )(coeffs, masked)
    return out.reshape(spectrum.shape)


def per_device(
    spectrum,
    legendre,
    order_of_slot,
    reduced_length,
    gauss_weight,
    depart_row,
    depart_col,
    depart_weight,
):
    own_index = lax.axis_index("wave")
    count = lax.axis_size("wave")
    slot_count = legendre.shape[0]
    orders_total = order_of_slot.shape[0]
    variables, level_count = spectrum.shape[:2]
    assert level_count == 1
    steps = depart_row.shape[0]
    grid_width = depart_row.shape[-1]
    stencil = depart_row.shape[2]
    fields = variables
    real_blocks = grid_width // BLOCK
    blocks = padded_blocks(grid_width)

    fits = slot_count % GROUP == 0 and 2 * fields == 8 and real_blocks <= 12
    if fits and legendre.shape[1] == 8 and count == 8:
        return fused(
            spectrum, legendre, order_of_slot, reduced_length, gauss_weight,
            depart_row, depart_col, depart_weight, count,
        )

    length = lax.dynamic_index_in_dim(reduced_length, own_index, keepdims=False)
    own_orders = lax.dynamic_slice_in_dim(order_of_slot, own_index * slot_count, slot_count)
    degrees = jnp.arange(legendre.shape[2], dtype=jnp.int32)
    masked = jnp.where(
        degrees[None, None, :] >= own_orders[:, None, None], legendre, jnp.zeros((), BF16)
    )
    order_limit = jnp.minimum(orders_total, (length - 1) // 2)
    cos_rows, sin_rows = phase_rows(length, order_of_slot, blocks)
    active = (order_of_slot < order_limit).astype(F32)[None, :]
    fc, fs = pl.pallas_call(
        build_table,
        out_shape=[jax.ShapeDtypeStruct((BLOCK, orders_total), BF16)] * 2,
        in_specs=[VMEM_SPEC] * 3,
        out_specs=[VMEM_SPEC] * 2,
        scratch_shapes=[pltpu.VMEM((RADIX * RADIX, orders_total), F32)] * 2,
        name="table",
    )(cos_rows, sin_rows, active)
    length1 = length.reshape(1)
    grid_scale = (1.0 / jnp.sqrt(order_limit.astype(F32))).reshape(1)
    coef_scale = (gauss_weight[0] * jnp.sqrt(2.0 / length.astype(F32))).reshape(1)

    synth = pl.pallas_call(
        functools.partial(synth_kernel, blocks),
        out_shape=jax.ShapeDtypeStruct((fields * blocks, BLOCK), BF16),
        in_specs=[VMEM_SPEC] * 5 + [SMEM_SPEC] * 2,
        out_specs=VMEM_SPEC,
        name="synth",
    )
    grid_step = pl.pallas_call(
        functools.partial(grid_kernel, fields, blocks, real_blocks),
        out_shape=jax.ShapeDtypeStruct((2 * fields, orders_total), BF16),
        in_specs=[VMEM_SPEC] * 8 + [SMEM_SPEC] * 2,
        out_specs=VMEM_SPEC,
        scratch_shapes=[pltpu.VMEM((fields * blocks, BLOCK), F32)],
        name="grid_step",
    )
    spectral = spectrum.reshape(2 * fields, slot_count, -1)
    fourier = jnp.einsum("vsn,sjn->jvs", spectral, masked, preferred_element_type=F32)
    gram = jnp.einsum("sjn,skn->sjk", masked, masked, preferred_element_type=F32)
    forward = [(i, i + 1) for i in range(count - 1)]
    backward = [(i + 1, i) for i in range(count - 1)]
    for k in range(steps):
        gathered = lax.all_to_all(fourier.astype(BF16), "wave", split_axis=0, concat_axis=2, tiled=True)
        own = synth(
            gathered.reshape(2 * fields, orders_total), cos_rows, sin_rows, fc, fs, length1, grid_scale
        )
        low = lax.ppermute(own, "wave", forward)
        high = lax.ppermute(own, "wave", backward)
        coeffs = grid_step(
            jnp.concatenate([low, own, high], axis=0),
            depart_row[k].reshape(1, stencil, 1, grid_width),
            depart_col[k].reshape(1, stencil, 1, grid_width),
            depart_weight[k].reshape(1, stencil, 1, grid_width),
            cos_rows, sin_rows, fc, fs, length1, coef_scale,
        )
        returned = lax.all_to_all(
            coeffs.reshape(1, 2 * fields, orders_total), "wave", split_axis=2, concat_axis=0, tiled=True
        )
        if k + 1 < steps:
            fourier = jnp.einsum("jvs,sjk->kvs", returned.astype(F32), gram, precision="highest")
    final = jnp.einsum("jvs,sjn->vsn", returned, masked, preferred_element_type=F32).astype(BF16)
    return final.reshape(spectrum.shape)


def solution(mesh):
    placed = (
        P(None, "lev", None, "wave", None),
        P("wave", None, None),
        P(),
        P(),
        P("wave"),
        P(None, "lev", None, "wave", None),
        P(None, "lev", None, "wave", None),
        P(None, "lev", None, "wave", None),
    )
    return jax.shard_map(
        per_device,
        mesh=mesh,
        in_specs=placed,
        out_specs=P(None, "lev", None, "wave", None),
        check_vma=False,
    )
```

```python
import functools
import math

import jax
import jax.numpy as jnp
from jax import lax
from jax.experimental import pallas as pl
from jax.experimental.pallas import tpu as pltpu
from jax.sharding import PartitionSpec as P

BLOCK = 512
RADIX = 8
FULL_TURN = 2.0 * math.pi
F32 = jnp.float32
BF16 = jnp.bfloat16

VMEM_SPEC = pl.BlockSpec(memory_space=pltpu.VMEM)
SMEM_SPEC = pl.BlockSpec(memory_space=pltpu.SMEM)


def padded_blocks(grid_width):
    return -(-(grid_width // BLOCK) // 16) * 16


def phase_rows(length, orders, blocks):
    digits = jnp.arange(RADIX, dtype=jnp.int32)
    steps = [digits, digits * RADIX, digits * RADIX * RADIX]
    steps.append(jnp.arange(blocks, dtype=jnp.int32) * BLOCK)
    steps = jnp.concatenate(steps)
    phases = steps[:, None] * orders[None, :] % length
    angles = phases.astype(F32) * (jnp.float32(FULL_TURN) / length.astype(F32))
    return jnp.cos(angles), jnp.sin(angles)


def build_table(cos_ref, sin_ref, active_ref, fc_ref, fs_ref, ca_ref, sa_ref):
    active = active_ref[...]
    cos_low = cos_ref[0:RADIX, :] * active
    sin_low = sin_ref[0:RADIX, :] * active
    cos_mid = cos_ref[RADIX : 2 * RADIX, :]
    sin_mid = sin_ref[RADIX : 2 * RADIX, :]
    for a in range(RADIX):
        c = cos_ref[2 * RADIX + a : 2 * RADIX + a + 1, :]
        s = sin_ref[2 * RADIX + a : 2 * RADIX + a + 1, :]
        ca_ref[a * RADIX : (a + 1) * RADIX, :] = c * cos_mid - s * sin_mid
        sa_ref[a * RADIX : (a + 1) * RADIX, :] = s * cos_mid + c * sin_mid

    def body(i, carry):
        cos_parts, sin_parts = [], []
        for k in range(2):
            c = ca_ref[pl.ds(2 * i + k, 1), :]
            s = sa_ref[pl.ds(2 * i + k, 1), :]
            cos_parts.append(c * cos_low - s * sin_low)
            sin_parts.append(-(s * cos_low + c * sin_low))
        rows = pl.ds(pl.multiple_of(i * 2 * RADIX, 2 * RADIX), 2 * RADIX)
        fc_ref[rows, :] = jnp.concatenate(cos_parts, axis=0).astype(BF16)
        fs_ref[rows, :] = jnp.concatenate(sin_parts, axis=0).astype(BF16)
        return carry

    lax.fori_loop(0, RADIX * RADIX // 2, body, 0)


def synthesize(coeffs, cos_block, sin_block, fc_ref, fs_ref, length, scale):
    fields = coeffs.shape[0] // 2
    blocks = cos_block.shape[0]
    reals, imags = [], []
    for v in range(fields):
        real = coeffs[2 * v : 2 * v + 1]
        imag = coeffs[2 * v + 1 : 2 * v + 2]
        reals.append((real * cos_block - imag * sin_block).astype(BF16))
        imags.append((real * sin_block + imag * cos_block).astype(BF16))
    dims = (((1,), (1,)), ((), ()))
    out = lax.dot_general(
        jnp.concatenate(reals, axis=0), fc_ref[...], dims, preferred_element_type=F32
    ) + lax.dot_general(
        jnp.concatenate(imags, axis=0), fs_ref[...], dims, preferred_element_type=F32
    )
    row = lax.broadcasted_iota(jnp.int32, out.shape, 0) % blocks
    point = row * BLOCK + lax.broadcasted_iota(jnp.int32, out.shape, 1)
    return jnp.where(point < length, out * scale, 0.0)


def synth_kernel(blocks, coef_ref, cos_ref, sin_ref, fc_ref, fs_ref, len_ref, scale_ref, out_ref):
    out_ref[...] = synthesize(
        coef_ref[...].astype(F32),
        cos_ref[3 * RADIX : 3 * RADIX + blocks, :],
        sin_ref[3 * RADIX : 3 * RADIX + blocks, :],
        fc_ref,
        fs_ref,
        len_ref[0],
        scale_ref[0],
    ).astype(BF16)


def gather_block(b, k, table, row_ref, col_ref, weight_ref, fields, blocks):
    stencil = col_ref.shape[1]
    half = 256
    lanes = pl.ds(pl.multiple_of(b * BLOCK, BLOCK), BLOCK)
    iota_half = lax.broadcasted_iota(jnp.int32, (half, BLOCK), 0).astype(F32).astype(BF16)
    iota_rows = lax.broadcasted_iota(jnp.int32, (3 * blocks, BLOCK), 0)
    one = jnp.ones((), BF16)
    zero = jnp.zeros((), BF16)
    acc = [jnp.zeros((blocks, BLOCK), F32) for _ in range(fields)]
    for p in range(stencil):
        col = col_ref[k, p, :, lanes]
        row = row_ref[k, p, :, lanes]
        weight = weight_ref[k, p, :, lanes]
        point = col % BLOCK
        halves = []
        for h in range(BLOCK // half):
            local = point - h * half
            key = jnp.where((local >= 0) & (local < half), local, -1).astype(F32).astype(BF16)
            halves.append(jnp.where(iota_half == key, one, zero))
        onehot = jnp.concatenate(halves, axis=0)
        found = jnp.dot(table, onehot, preferred_element_type=F32)
        which = (row + 1) * blocks + col // BLOCK
        chosen = jnp.where(iota_rows == which, weight, 0.0)
        for r in range(3):
            sel = chosen[r * blocks : (r + 1) * blocks]
            for v in range(fields):
                start = (r * fields + v) * blocks
                acc[v] = acc[v] + found[start : start + blocks] * sel
    return [jnp.sum(a, axis=0, keepdims=True) for a in acc]


def advance(table, k, row_ref, col_ref, weight_ref, new_ref, length, fields, blocks, real_blocks):
    new_ref[...] = jnp.zeros_like(new_ref)

    def body(b, carry):
        interp = gather_block(b, k, table, row_ref, col_ref, weight_ref, fields, blocks)
        point = b * BLOCK + lax.broadcasted_iota(jnp.int32, (1, BLOCK), 1)
        for v in range(fields):
            value = interp[v] + 0.5 * interp[(v + 1) % fields] * jnp.tanh(interp[(v + 2) % fields])
            new_ref[pl.ds(v * blocks + b, 1), :] = jnp.where(point < length, value, 0.0)
        return carry

    lax.fori_loop(0, real_blocks, body, 0)


def analyse(new_ref, cos_block, sin_block, fc_ref, fs_ref, scale):
    blocks = cos_block.shape[0]
    fields = new_ref.shape[0] // blocks
    newgrid = new_ref[...].astype(BF16)
    part_real = jnp.dot(newgrid, fc_ref[...], preferred_element_type=F32)
    part_imag = jnp.dot(newgrid, fs_ref[...], preferred_element_type=F32)
    out = []
    for v in range(fields):
        pr = part_real[v * blocks : (v + 1) * blocks]
        pi = part_imag[v * blocks : (v + 1) * blocks]
        real = jnp.sum(pr * cos_block + pi * sin_block, axis=0, keepdims=True)
        imag = jnp.sum(pi * cos_block - pr * sin_block, axis=0, keepdims=True)
        out += [real * scale, imag * scale]
    return out


def grid_kernel(
    fields, blocks, real_blocks,
    table_ref, row_ref, col_ref, weight_ref, cos_ref, sin_ref, fc_ref, fs_ref, len_ref, scale_ref,
    out_ref, new_ref,
):
    advance(
        table_ref[...], 0, row_ref, col_ref, weight_ref, new_ref, len_ref[0],
        fields, blocks, real_blocks,
    )
    rows = analyse(
        new_ref,
        cos_ref[3 * RADIX : 3 * RADIX + blocks, :],
        sin_ref[3 * RADIX : 3 * RADIX + blocks, :],
        fc_ref,
        fs_ref,
        scale_ref[0],
    )
    out_ref[...] = jnp.concatenate(rows, axis=0).astype(BF16)


HALF = 256


def fill_phases(orders, length, cos_ref, sin_ref):
    limit = length.astype(F32)
    inverse = 1.0 / jnp.full(orders.shape, limit)
    turn = FULL_TURN / jnp.full(orders.shape, limit)
    digit = lax.broadcasted_iota(jnp.int32, (RADIX, orders.shape[1]), 0)
    for t in range(cos_ref.shape[0] // RADIX):
        if t < 3:
            step = digit * RADIX**t
        else:
            step = (digit + (t - 3) * RADIX) * BLOCK
        product = step * orders
        rest = product - jnp.floor(product.astype(F32) * inverse).astype(jnp.int32) * length
        rest = jnp.where(rest < 0, rest + length, rest)
        rest = jnp.where(rest >= length, rest - length, rest)
        angle = rest.astype(F32) * turn
        cos_ref[t * RADIX : (t + 1) * RADIX, :] = jnp.cos(angle)
        sin_ref[t * RADIX : (t + 1) * RADIX, :] = jnp.sin(angle)


def grid_rows(coeffs, cos_block, sin_block, fc_ref, fs_ref, length, scale):
    fields = coeffs.shape[0] // 2
    blocks = cos_block.shape[0]
    reals, imags = [], []
    for v in range(fields):
        real = coeffs[2 * v : 2 * v + 1]
        imag = coeffs[2 * v + 1 : 2 * v + 2]
        reals.append((real * cos_block - imag * sin_block).astype(BF16))
        imags.append((real * sin_block + imag * cos_block).astype(BF16))
    dims = (((1,), (1,)), ((), ()))
    out = lax.dot_general(
        fc_ref[...], jnp.concatenate(reals, axis=0), dims, preferred_element_type=F32
    ) + lax.dot_general(
        fs_ref[...], jnp.concatenate(imags, axis=0), dims, preferred_element_type=F32
    )
    out = out.T
    row = lax.broadcasted_iota(jnp.int32, out.shape, 0) % blocks
    point = row * BLOCK + lax.broadcasted_iota(jnp.int32, out.shape, 1)
    out = jnp.where(point < length, out * scale, 0.0)
    parts = []
    for v in range(fields):
        rows = out[v * blocks : (v + 1) * blocks]
        parts += [rows[:8, :HALF], rows[:8, HALF:], rows[8:12, :HALF], rows[8:12, HALF:]]
    return jnp.concatenate(parts, axis=0)


def pick_block(b, k, table, row_ref, col_ref, weight_ref, fields):
    stencil = col_ref.shape[1]
    lanes = pl.ds(pl.multiple_of(b * BLOCK, BLOCK), BLOCK)
    iota = lax.broadcasted_iota(jnp.int32, (HALF, BLOCK), 0).astype(F32).astype(BF16)
    sub = lax.broadcasted_iota(jnp.int32, (8, BLOCK), 0)
    one = jnp.ones((), BF16)
    zero = jnp.zeros((), BF16)
    acc = [jnp.zeros((8, BLOCK), F32) for _ in range(fields)]
    for p in range(stencil):
        col = col_ref[k, p, :, lanes]
        row = row_ref[k, p, :, lanes]
        weight = weight_ref[k, p, :, lanes]
        key = (col & (HALF - 1)).astype(F32).astype(BF16)
        onehot = jnp.where(iota == key, one, zero)
        found = jnp.dot(table, onehot, preferred_element_type=F32)
        big = col // BLOCK
        side = (col // HALF) & 1
        which = (row + 1) * 24 + jnp.where(big < 8, side * 8 + big, 8 + side * 4 + big)
        got = [jnp.zeros((8, BLOCK), F32) for _ in range(fields)]
        for r in range(3):
            for t in range(3):
                hit = sub == which - (r * 24 + t * 8)
                for v in range(fields):
                    start = (r * fields + v) * 24 + t * 8
                    got[v] = jnp.where(hit, found[start : start + 8], got[v])
        for v in range(fields):
            acc[v] = acc[v] + got[v] * weight
    return [jnp.sum(a, axis=0, keepdims=True) for a in acc]


def advance_fast(table, k, row_ref, col_ref, weight_ref, new_ref, length, fields, blocks, real_blocks):
    new_ref[...] = jnp.zeros_like(new_ref)

    def body(b, carry):
        interp = pick_block(b, k, table, row_ref, col_ref, weight_ref, fields)
        point = b * BLOCK + lax.broadcasted_iota(jnp.int32, (1, BLOCK), 1)
        for v in range(fields):
            value = interp[v] + 0.5 * interp[(v + 1) % fields] * jnp.tanh(interp[(v + 2) % fields])
            new_ref[pl.ds(v * blocks + b, 1), :] = jnp.where(point < length, value, 0.0)
        return carry

    lax.fori_loop(0, real_blocks, body, 0)


GROUP = 16
MESH = pl.DeviceIdType.MESH


def mask_group(g, first, orders_ref, leg_ref, rows_j):
    degree = lax.broadcasted_iota(jnp.int32, (rows_j, leg_ref.shape[2]), 1)
    for pair in range(GROUP // 2):
        rows = slice(2 * pair * rows_j, 2 * (pair + 1) * rows_j)
        both = leg_ref[g, rows, :].astype(F32)
        parts = []
        for s in range(2):
            keep = degree >= orders_ref[first + g * GROUP + 2 * pair + s]
            parts.append(jnp.where(keep, both[s * rows_j : (s + 1) * rows_j], 0.0))
        leg_ref[g, rows, :] = jnp.concatenate(parts, axis=0).astype(BF16)


def forward_group(g, fields, rows_j, spec_ref, leg_ref, four_ref, square_ref):
    masked = leg_ref[g]
    state = spec_ref[g].reshape(fields * GROUP, spec_ref.shape[3])
    both = lax.dot_general(
        masked, jnp.concatenate([state, masked], axis=0), (((1,), (1,)), ((), ())),
        preferred_element_type=F32,
    )
    size = GROUP * rows_j
    width = fields * GROUP
    row = lax.broadcasted_iota(jnp.int32, (size, width), 0) // rows_j
    col = lax.broadcasted_iota(jnp.int32, (size, width), 1) % GROUP
    prod = jnp.where(row == col, both[:, :width], 0.0)
    four_ref[g] = jnp.sum(prod.reshape(GROUP, rows_j, width), axis=0)
    row = lax.broadcasted_iota(jnp.int32, (size, size), 0)
    col = lax.broadcasted_iota(jnp.int32, (size, size), 1)
    square = jnp.where(row // rows_j == col // rows_j, both[:, width:], 0.0)
    square_ref[g] = jnp.sum(square.reshape(GROUP, rows_j, size), axis=0)


def gram_of(square_ref, gram_ref, rows_j):
    groups, _, size = square_ref.shape
    row = lax.broadcasted_iota(jnp.int32, (size, size), 0)
    col = lax.broadcasted_iota(jnp.int32, (size, size), 1)
    swap = (row // rows_j == col % GROUP) & (row % rows_j == col // GROUP)
    turned = jnp.dot(
        square_ref[...].reshape(groups * rows_j, size), jnp.where(swap, 1.0, 0.0),
        preferred_element_type=F32, precision="highest",
    )
    gram_ref[...] = jnp.zeros_like(gram_ref)
    for h in range(groups):
        rows = turned[h * rows_j : (h + 1) * rows_j]
        for j in range(rows_j):
            gram_ref[j, :, h * GROUP : (h + 1) * GROUP] = rows[:, j * GROUP : (j + 1) * GROUP]


def inverse_group(g, fields, rows_j, coef_ref, leg_ref, out_ref):
    size = GROUP * rows_j
    row = lax.broadcasted_iota(jnp.int32, (size, fields * GROUP), 0) // rows_j
    col = lax.broadcasted_iota(jnp.int32, (size, fields * GROUP), 1) % GROUP
    tiled = jnp.concatenate([coef_ref[g]] * GROUP, axis=0)
    spread = jnp.where(row == col, tiled, 0.0).T.astype(BF16)
    out = jnp.dot(spread, leg_ref[g], preferred_element_type=F32)
    out_ref[g] = out.astype(BF16).reshape(out_ref.shape[1:])


def steps_kernel(
    steps, count, fields, blocks, real_blocks, slots,
    spec_hbm, leg_hbm, orders_ref, row_ref, col_ref, weight_ref, order_ref, len_ref, gauss_ref,
    out_hbm,
    spec_ref, leg_ref, four_ref, square_ref, vjs_ref, first_ref, gram_ref, load_sem, out_sem,
    cos_ref, sin_ref, fc_ref, fs_ref, ca_ref, sa_ref, spec_send, spec_recv, grid_send, grid_recv, tab_ref, coef_ref,
    new_ref, spec_ssem, spec_rsem, grid_ssem, grid_rsem, halo_ssem, halo_rsem,
):
    rows_j = leg_ref.shape[1] // GROUP
    groups = slots // GROUP

    def loads(g):
        slot_rows = pl.ds(pl.multiple_of(g * GROUP, GROUP), GROUP)
        return (
            pltpu.make_async_copy(leg_hbm.at[g], leg_ref.at[g], load_sem.at[0, g]),
            pltpu.make_async_copy(spec_hbm.at[:, slot_rows, :], spec_ref.at[g], load_sem.at[1, g]),
        )

    def store(g):
        slot_rows = pl.ds(pl.multiple_of(g * GROUP, GROUP), GROUP)
        return pltpu.make_async_copy(spec_ref.at[g], out_hbm.at[:, slot_rows, :], out_sem.at[g])

    for g in range(groups):
        for copy in loads(g):
            copy.start()
    tab_ref[...] = jnp.zeros_like(tab_ref)
    vjs_ref[...] = jnp.zeros_like(vjs_ref)
    grid_send[...] = jnp.zeros_like(grid_send)
    me = lax.axis_index("wave")
    peers = [lax.rem(me + d, count) for d in range(1, count)]
    barrier = pltpu.get_barrier_semaphore()
    for peer in peers:
        pl.semaphore_signal(barrier, inc=1, device_id={"wave": peer}, device_id_type=MESH)
    length = len_ref[me]
    orders = orders_ref[...]
    limit = jnp.minimum(orders.shape[1], (length - 1) // 2)
    fill_phases(orders, length, cos_ref, sin_ref)

    def forward(g, carry):
        for copy in loads(g):
            copy.wait()
        mask_group(g, me * slots, order_ref, leg_ref, rows_j)
        forward_group(g, fields, rows_j, spec_ref, leg_ref, four_ref, square_ref)
        return carry

    lax.fori_loop(0, groups, forward, 0)
    for h in range(groups):
        for v in range(fields):
            vjs_ref[v, :, h * GROUP : (h + 1) * GROUP] = four_ref[
                h, :, v * GROUP : (v + 1) * GROUP
            ]
    first_ref[...] = jnp.swapaxes(vjs_ref[...], 0, 1)
    pl.semaphore_wait(barrier, count - 1)

    def exchange(send, recv, ssem, rsem):
        copies = []
        for d, peer in enumerate(peers):
            copy = pltpu.make_async_remote_copy(
                src_ref=send.at[peer], dst_ref=recv.at[me], send_sem=ssem.at[d],
                recv_sem=rsem.at[d], device_id={"wave": peer}, device_id_type=MESH,
            )
            copy.start()
            copies.append(copy)
        return copies

    copies = exchange(first_ref, spec_recv.at[0], spec_ssem.at[0], spec_rsem.at[0])
    gram_of(square_ref, gram_ref, rows_j)
    active = jnp.where(orders < limit, 1.0, 0.0)
    build_table(cos_ref, sin_ref, active, fc_ref, fs_ref, ca_ref, sa_ref)
    grid_scale = 1.0 / jnp.sqrt(jnp.full((1, BLOCK), limit.astype(F32)))
    coef_scale = gauss_ref[0] * jnp.sqrt(2.0 / jnp.full(orders.shape, length.astype(F32)))
    cos_block = cos_ref[3 * RADIX : 3 * RADIX + blocks, :]
    sin_block = sin_ref[3 * RADIX : 3 * RADIX + blocks, :]
    rows = fields // 2 * 24
    for k in range(steps):
        source = first_ref if k == 0 else spec_send.at[k - 1]
        for copy in copies:
            copy.wait()
        spec_recv[k, me] = source[me]
        for i in range(count):
            coef_ref[:, i * slots : (i + 1) * slots] = spec_recv[k, i, :, :slots]
        own = grid_rows(
            coef_ref[...], cos_block, sin_block, fc_ref, fs_ref, length, grid_scale
        )
        tab_ref[k, 1] = own.astype(BF16)
        up = pltpu.make_async_remote_copy(
            src_ref=tab_ref.at[k, 1], dst_ref=tab_ref.at[k, 0], send_sem=halo_ssem.at[k, 0],
            recv_sem=halo_rsem.at[k, 0], device_id={"wave": lax.rem(me + 1, count)},
            device_id_type=MESH,
        )
        down = pltpu.make_async_remote_copy(
            src_ref=tab_ref.at[k, 1], dst_ref=tab_ref.at[k, 2], send_sem=halo_ssem.at[k, 1],
            recv_sem=halo_rsem.at[k, 1], device_id={"wave": lax.rem(me + count - 1, count)},
            device_id_type=MESH,
        )

        @pl.when(me < count - 1)
        def _():
            up.start()

        @pl.when(me > 0)
        def _():
            down.start()
            up.wait_recv()

        @pl.when(me < count - 1)
        def _():
            down.wait_recv()

        table = tab_ref[k].reshape(3 * rows, HALF)
        advance_fast(
            table, k, row_ref, col_ref, weight_ref, new_ref, length,
            fields // 2, blocks, real_blocks,
        )

        @pl.when(me < count - 1)
        def _():
            up.wait_send()

        @pl.when(me > 0)
        def _():
            down.wait_send()

        parts = analyse(new_ref, cos_block, sin_block, fc_ref, fs_ref, coef_scale)
        for v, part in enumerate(parts):
            coef_ref[v : v + 1, :] = part
        for i in range(count):
            grid_send[k, i, :, :slots] = coef_ref[:, i * slots : (i + 1) * slots]
        copies = exchange(grid_send.at[k], grid_recv.at[k], grid_ssem.at[k], grid_rsem.at[k])
        grid_recv[k, me] = grid_send[k, me]
        for copy in copies:
            copy.wait()
        if k + 1 < steps:
            mixed = []
            for v in range(fields):
                total = None
                for j in range(count):
                    term = gram_ref[j] * grid_recv[k, j, v : v + 1, :]
                    total = term if total is None else total + term
                mixed.append(total[None])
            spec_send[k] = jnp.swapaxes(jnp.concatenate(mixed, axis=0), 0, 1)
            copies = exchange(
                spec_send.at[k], spec_recv.at[k + 1], spec_ssem.at[k + 1], spec_rsem.at[k + 1]
            )
    last = jnp.swapaxes(grid_recv[steps - 1], 0, 1)
    for h in range(slots // GROUP):
        for v in range(fields):
            four_ref[h, :, v * GROUP : (v + 1) * GROUP] = last[v, :, h * GROUP : (h + 1) * GROUP]

    def inverse(g, carry):
        inverse_group(g, fields, rows_j, four_ref, leg_ref, spec_ref)
        store(g).start()
        return carry

    lax.fori_loop(0, groups, inverse, 0)
    for g in range(groups):
        store(g).wait()


def fused(spectrum, legendre, order_of_slot, reduced_length, gauss_weight, row, col, weight, count):
    slots, rows_j, degrees = legendre.shape
    fields = 2 * spectrum.shape[0]
    orders_total = order_of_slot.shape[0]
    steps, stencil, grid_width = row.shape[0], row.shape[2], row.shape[-1]
    real_blocks = grid_width // BLOCK
    blocks = padded_blocks(grid_width)
    groups = slots // GROUP
    size = GROUP * rows_j
    lanes = -(-slots // 128) * 128
    shape = (steps, count, fields, lanes)
    table_rows = fields // 2 * blocks
    out = pl.pallas_call(
        functools.partial(steps_kernel, steps, count, fields, blocks, real_blocks, slots),
        out_shape=jax.ShapeDtypeStruct((fields, slots, degrees), BF16),
        in_specs=[pl.BlockSpec(memory_space=pl.ANY)] * 2 + [VMEM_SPEC] * 4 + [SMEM_SPEC] * 3,
        out_specs=pl.BlockSpec(memory_space=pl.ANY),
        scratch_shapes=[
            pltpu.VMEM((groups, fields, GROUP, degrees), BF16),
            pltpu.VMEM((groups, size, degrees), BF16),
            pltpu.VMEM((groups, rows_j, fields * GROUP), F32),
            pltpu.VMEM((groups, rows_j, size), F32),
            pltpu.VMEM((fields, rows_j, lanes), F32),
            pltpu.VMEM((rows_j, fields, lanes), F32),
            pltpu.VMEM((rows_j, rows_j, lanes), F32),
            pltpu.SemaphoreType.DMA((2, groups)),
            pltpu.SemaphoreType.DMA((groups,)),
        ]
        + [pltpu.VMEM((3 * RADIX + blocks, orders_total), F32)] * 2
        + [pltpu.VMEM((BLOCK, orders_total), BF16)] * 2
        + [pltpu.VMEM((RADIX * RADIX, orders_total), F32)] * 2
        + [pltpu.VMEM(shape, F32)] * 4
        + [
            pltpu.VMEM((steps, 3, fields // 2 * 24, HALF), BF16),
            pltpu.VMEM((fields, orders_total), F32),
            pltpu.VMEM((table_rows, BLOCK), F32),
        ]
        + [pltpu.SemaphoreType.DMA((steps, count - 1))] * 4
        + [pltpu.SemaphoreType.DMA((steps, 2))] * 2,
        compiler_params=pltpu.CompilerParams(collective_id=0, has_side_effects=True),
        name="steps",
    )(
        spectrum.reshape(fields, slots, degrees),
        legendre.reshape(groups, size, degrees),
        order_of_slot.reshape(1, orders_total),
        row.reshape(steps, stencil, 1, grid_width),
        col.reshape(steps, stencil, 1, grid_width),
        weight.reshape(steps, stencil, 1, grid_width),
        order_of_slot, reduced_length, gauss_weight,
    )
    return out.reshape(spectrum.shape)


def per_device(
    spectrum,
    legendre,
    order_of_slot,
    reduced_length,
    gauss_weight,
    depart_row,
    depart_col,
    depart_weight,
):
    own_index = lax.axis_index("wave")
    count = lax.axis_size("wave")
    slot_count = legendre.shape[0]
    orders_total = order_of_slot.shape[0]
    variables, level_count = spectrum.shape[:2]
    assert level_count == 1
    steps = depart_row.shape[0]
    grid_width = depart_row.shape[-1]
    stencil = depart_row.shape[2]
    fields = variables
    real_blocks = grid_width // BLOCK
    blocks = padded_blocks(grid_width)

    fits = slot_count % GROUP == 0 and 2 * fields == 8 and real_blocks <= 12
    if fits and legendre.shape[1] == 8 and count == 8:
        return fused(
            spectrum, legendre, order_of_slot, reduced_length, gauss_weight,
            depart_row, depart_col, depart_weight, count,
        )

    length = lax.dynamic_index_in_dim(reduced_length, own_index, keepdims=False)
    own_orders = lax.dynamic_slice_in_dim(order_of_slot, own_index * slot_count, slot_count)
    degrees = jnp.arange(legendre.shape[2], dtype=jnp.int32)
    masked = jnp.where(
        degrees[None, None, :] >= own_orders[:, None, None], legendre, jnp.zeros((), BF16)
    )
    order_limit = jnp.minimum(orders_total, (length - 1) // 2)
    cos_rows, sin_rows = phase_rows(length, order_of_slot, blocks)
    active = (order_of_slot < order_limit).astype(F32)[None, :]
    fc, fs = pl.pallas_call(
        build_table,
        out_shape=[jax.ShapeDtypeStruct((BLOCK, orders_total), BF16)] * 2,
        in_specs=[VMEM_SPEC] * 3,
        out_specs=[VMEM_SPEC] * 2,
        scratch_shapes=[pltpu.VMEM((RADIX * RADIX, orders_total), F32)] * 2,
        name="table",
    )(cos_rows, sin_rows, active)
    length1 = length.reshape(1)
    grid_scale = (1.0 / jnp.sqrt(order_limit.astype(F32))).reshape(1)
    coef_scale = (gauss_weight[0] * jnp.sqrt(2.0 / length.astype(F32))).reshape(1)

    synth = pl.pallas_call(
        functools.partial(synth_kernel, blocks),
        out_shape=jax.ShapeDtypeStruct((fields * blocks, BLOCK), BF16),
        in_specs=[VMEM_SPEC] * 5 + [SMEM_SPEC] * 2,
        out_specs=VMEM_SPEC,
        name="synth",
    )
    grid_step = pl.pallas_call(
        functools.partial(grid_kernel, fields, blocks, real_blocks),
        out_shape=jax.ShapeDtypeStruct((2 * fields, orders_total), BF16),
        in_specs=[VMEM_SPEC] * 8 + [SMEM_SPEC] * 2,
        out_specs=VMEM_SPEC,
        scratch_shapes=[pltpu.VMEM((fields * blocks, BLOCK), F32)],
        name="grid_step",
    )
    spectral = spectrum.reshape(2 * fields, slot_count, -1)
    fourier = jnp.einsum("vsn,sjn->jvs", spectral, masked, preferred_element_type=F32)
    gram = jnp.einsum("sjn,skn->sjk", masked, masked, preferred_element_type=F32)
    forward = [(i, i + 1) for i in range(count - 1)]
    backward = [(i + 1, i) for i in range(count - 1)]
    for k in range(steps):
        gathered = lax.all_to_all(fourier.astype(BF16), "wave", split_axis=0, concat_axis=2, tiled=True)
        own = synth(
            gathered.reshape(2 * fields, orders_total), cos_rows, sin_rows, fc, fs, length1, grid_scale
        )
        low = lax.ppermute(own, "wave", forward)
        high = lax.ppermute(own, "wave", backward)
        coeffs = grid_step(
            jnp.concatenate([low, own, high], axis=0),
            depart_row[k].reshape(1, stencil, 1, grid_width),
            depart_col[k].reshape(1, stencil, 1, grid_width),
            depart_weight[k].reshape(1, stencil, 1, grid_width),
            cos_rows, sin_rows, fc, fs, length1, coef_scale,
        )
        returned = lax.all_to_all(
            coeffs.reshape(1, 2 * fields, orders_total), "wave", split_axis=2, concat_axis=0, tiled=True
        )
        if k + 1 < steps:
            fourier = jnp.einsum("jvs,sjk->kvs", returned.astype(F32), gram, precision="highest")
    final = jnp.einsum("jvs,sjn->vsn", returned, masked, preferred_element_type=F32).astype(BF16)
    return final.reshape(spectrum.shape)


def solution(mesh):
    placed = (
        P(None, "lev", None, "wave", None),
        P("wave", None, None),
        P(),
        P(),
        P("wave"),
        P(None, "lev", None, "wave", None),
        P(None, "lev", None, "wave", None),
        P(None, "lev", None, "wave", None),
    )
    return jax.shard_map(
        per_device,
        mesh=mesh,
        in_specs=placed,
        out_specs=P(None, "lev", None, "wave", None),
        check_vma=False,
    )
```

```python
import functools
import math

import jax
import jax.numpy as jnp
from jax import lax
from jax.experimental import pallas as pl
from jax.experimental.pallas import tpu as pltpu
from jax.sharding import PartitionSpec as P

BLOCK = 512
RADIX = 8
FULL_TURN = 2.0 * math.pi
F32 = jnp.float32
BF16 = jnp.bfloat16

VMEM_SPEC = pl.BlockSpec(memory_space=pltpu.VMEM)
SMEM_SPEC = pl.BlockSpec(memory_space=pltpu.SMEM)


def padded_blocks(grid_width):
    return -(-(grid_width // BLOCK) // 16) * 16


def phase_rows(length, orders, blocks):
    digits = jnp.arange(RADIX, dtype=jnp.int32)
    steps = [digits, digits * RADIX, digits * RADIX * RADIX]
    steps.append(jnp.arange(blocks, dtype=jnp.int32) * BLOCK)
    steps = jnp.concatenate(steps)
    phases = steps[:, None] * orders[None, :] % length
    angles = phases.astype(F32) * (jnp.float32(FULL_TURN) / length.astype(F32))
    return jnp.cos(angles), jnp.sin(angles)


def build_table(cos_ref, sin_ref, active_ref, fc_ref, fs_ref, ca_ref, sa_ref):
    active = active_ref[...]
    cos_low = cos_ref[0:RADIX, :] * active
    sin_low = sin_ref[0:RADIX, :] * active
    cos_mid = cos_ref[RADIX : 2 * RADIX, :]
    sin_mid = sin_ref[RADIX : 2 * RADIX, :]
    for a in range(RADIX):
        c = cos_ref[2 * RADIX + a : 2 * RADIX + a + 1, :]
        s = sin_ref[2 * RADIX + a : 2 * RADIX + a + 1, :]
        ca_ref[a * RADIX : (a + 1) * RADIX, :] = c * cos_mid - s * sin_mid
        sa_ref[a * RADIX : (a + 1) * RADIX, :] = s * cos_mid + c * sin_mid

    def body(i, carry):
        cos_parts, sin_parts = [], []
        for k in range(2):
            c = ca_ref[pl.ds(2 * i + k, 1), :]
            s = sa_ref[pl.ds(2 * i + k, 1), :]
            cos_parts.append(c * cos_low - s * sin_low)
            sin_parts.append(-(s * cos_low + c * sin_low))
        rows = pl.ds(pl.multiple_of(i * 2 * RADIX, 2 * RADIX), 2 * RADIX)
        fc_ref[rows, :] = jnp.concatenate(cos_parts, axis=0).astype(BF16)
        fs_ref[rows, :] = jnp.concatenate(sin_parts, axis=0).astype(BF16)
        return carry

    lax.fori_loop(0, RADIX * RADIX // 2, body, 0)


def synthesize(coeffs, cos_block, sin_block, fc_ref, fs_ref, length, scale):
    fields = coeffs.shape[0] // 2
    blocks = cos_block.shape[0]
    reals, imags = [], []
    for v in range(fields):
        real = coeffs[2 * v : 2 * v + 1]
        imag = coeffs[2 * v + 1 : 2 * v + 2]
        reals.append((real * cos_block - imag * sin_block).astype(BF16))
        imags.append((real * sin_block + imag * cos_block).astype(BF16))
    dims = (((1,), (1,)), ((), ()))
    out = lax.dot_general(
        jnp.concatenate(reals, axis=0), fc_ref[...], dims, preferred_element_type=F32
    ) + lax.dot_general(
        jnp.concatenate(imags, axis=0), fs_ref[...], dims, preferred_element_type=F32
    )
    row = lax.broadcasted_iota(jnp.int32, out.shape, 0) % blocks
    point = row * BLOCK + lax.broadcasted_iota(jnp.int32, out.shape, 1)
    return jnp.where(point < length, out * scale, 0.0)


def synth_kernel(blocks, coef_ref, cos_ref, sin_ref, fc_ref, fs_ref, len_ref, scale_ref, out_ref):
    out_ref[...] = synthesize(
        coef_ref[...].astype(F32),
        cos_ref[3 * RADIX : 3 * RADIX + blocks, :],
        sin_ref[3 * RADIX : 3 * RADIX + blocks, :],
        fc_ref,
        fs_ref,
        len_ref[0],
        scale_ref[0],
    ).astype(BF16)


def gather_block(b, k, table, row_ref, col_ref, weight_ref, fields, blocks):
    stencil = col_ref.shape[1]
    half = 256
    lanes = pl.ds(pl.multiple_of(b * BLOCK, BLOCK), BLOCK)
    iota_half = lax.broadcasted_iota(jnp.int32, (half, BLOCK), 0).astype(F32).astype(BF16)
    iota_rows = lax.broadcasted_iota(jnp.int32, (3 * blocks, BLOCK), 0)
    one = jnp.ones((), BF16)
    zero = jnp.zeros((), BF16)
    acc = [jnp.zeros((blocks, BLOCK), F32) for _ in range(fields)]
    for p in range(stencil):
        col = col_ref[k, p, :, lanes]
        row = row_ref[k, p, :, lanes]
        weight = weight_ref[k, p, :, lanes]
        point = col % BLOCK
        halves = []
        for h in range(BLOCK // half):
            local = point - h * half
            key = jnp.where((local >= 0) & (local < half), local, -1).astype(F32).astype(BF16)
            halves.append(jnp.where(iota_half == key, one, zero))
        onehot = jnp.concatenate(halves, axis=0)
        found = jnp.dot(table, onehot, preferred_element_type=F32)
        which = (row + 1) * blocks + col // BLOCK
        chosen = jnp.where(iota_rows == which, weight, 0.0)
        for r in range(3):
            sel = chosen[r * blocks : (r + 1) * blocks]
            for v in range(fields):
                start = (r * fields + v) * blocks
                acc[v] = acc[v] + found[start : start + blocks] * sel
    return [jnp.sum(a, axis=0, keepdims=True) for a in acc]


def advance(table, k, row_ref, col_ref, weight_ref, new_ref, length, fields, blocks, real_blocks):
    new_ref[...] = jnp.zeros_like(new_ref)

    def body(b, carry):
        interp = gather_block(b, k, table, row_ref, col_ref, weight_ref, fields, blocks)
        point = b * BLOCK + lax.broadcasted_iota(jnp.int32, (1, BLOCK), 1)
        for v in range(fields):
            value = interp[v] + 0.5 * interp[(v + 1) % fields] * jnp.tanh(interp[(v + 2) % fields])
            new_ref[pl.ds(v * blocks + b, 1), :] = jnp.where(point < length, value, 0.0)
        return carry

    lax.fori_loop(0, real_blocks, body, 0)


def analyse(new_ref, cos_block, sin_block, fc_ref, fs_ref, scale):
    blocks = cos_block.shape[0]
    fields = new_ref.shape[0] // blocks
    newgrid = new_ref[...].astype(BF16)
    part_real = jnp.dot(newgrid, fc_ref[...], preferred_element_type=F32)
    part_imag = jnp.dot(newgrid, fs_ref[...], preferred_element_type=F32)
    out = []
    for v in range(fields):
        pr = part_real[v * blocks : (v + 1) * blocks]
        pi = part_imag[v * blocks : (v + 1) * blocks]
        real = jnp.sum(pr * cos_block + pi * sin_block, axis=0, keepdims=True)
        imag = jnp.sum(pi * cos_block - pr * sin_block, axis=0, keepdims=True)
        out += [real * scale, imag * scale]
    return out


def grid_kernel(
    fields, blocks, real_blocks,
    table_ref, row_ref, col_ref, weight_ref, cos_ref, sin_ref, fc_ref, fs_ref, len_ref, scale_ref,
    out_ref, new_ref,
):
    advance(
        table_ref[...], 0, row_ref, col_ref, weight_ref, new_ref, len_ref[0],
        fields, blocks, real_blocks,
    )
    rows = analyse(
        new_ref,
        cos_ref[3 * RADIX : 3 * RADIX + blocks, :],
        sin_ref[3 * RADIX : 3 * RADIX + blocks, :],
        fc_ref,
        fs_ref,
        scale_ref[0],
    )
    out_ref[...] = jnp.concatenate(rows, axis=0).astype(BF16)


HALF = 256


def fill_phases(orders, length, cos_ref, sin_ref):
    limit = length.astype(F32)
    inverse = 1.0 / jnp.full(orders.shape, limit)
    turn = FULL_TURN / jnp.full(orders.shape, limit)
    digit = lax.broadcasted_iota(jnp.int32, (RADIX, orders.shape[1]), 0)
    for t in range(cos_ref.shape[0] // RADIX):
        if t < 3:
            step = digit * RADIX**t
        else:
            step = (digit + (t - 3) * RADIX) * BLOCK
        product = step * orders
        rest = product - jnp.floor(product.astype(F32) * inverse).astype(jnp.int32) * length
        rest = jnp.where(rest < 0, rest + length, rest)
        rest = jnp.where(rest >= length, rest - length, rest)
        angle = rest.astype(F32) * turn
        cos_ref[t * RADIX : (t + 1) * RADIX, :] = jnp.cos(angle)
        sin_ref[t * RADIX : (t + 1) * RADIX, :] = jnp.sin(angle)


def grid_rows(coeffs, cos_block, sin_block, fc_ref, fs_ref, length, scale):
    fields = coeffs.shape[0] // 2
    blocks = cos_block.shape[0]
    reals, imags = [], []
    for v in range(fields):
        real = coeffs[2 * v : 2 * v + 1]
        imag = coeffs[2 * v + 1 : 2 * v + 2]
        reals.append((real * cos_block - imag * sin_block).astype(BF16))
        imags.append((real * sin_block + imag * cos_block).astype(BF16))
    dims = (((1,), (1,)), ((), ()))
    out = lax.dot_general(
        fc_ref[...], jnp.concatenate(reals, axis=0), dims, preferred_element_type=F32
    ) + lax.dot_general(
        fs_ref[...], jnp.concatenate(imags, axis=0), dims, preferred_element_type=F32
    )
    out = out.T
    row = lax.broadcasted_iota(jnp.int32, out.shape, 0) % blocks
    point = row * BLOCK + lax.broadcasted_iota(jnp.int32, out.shape, 1)
    out = jnp.where(point < length, out * scale, 0.0)
    parts = []
    for v in range(fields):
        rows = out[v * blocks : (v + 1) * blocks]
        parts += [rows[:8, :HALF], rows[:8, HALF:], rows[8:12, :HALF], rows[8:12, HALF:]]
    return jnp.concatenate(parts, axis=0)


def pick_block(b, k, table, row_ref, col_ref, weight_ref, fields):
    stencil = col_ref.shape[1]
    lanes = pl.ds(pl.multiple_of(b * BLOCK, BLOCK), BLOCK)
    iota = lax.broadcasted_iota(jnp.int32, (HALF, BLOCK), 0).astype(F32).astype(BF16)
    sub = lax.broadcasted_iota(jnp.int32, (8, BLOCK), 0)
    one = jnp.ones((), BF16)
    zero = jnp.zeros((), BF16)
    acc = [jnp.zeros((8, BLOCK), F32) for _ in range(fields)]
    for p in range(stencil):
        col = col_ref[k, p, :, lanes]
        row = row_ref[k, p, :, lanes]
        weight = weight_ref[k, p, :, lanes]
        key = (col & (HALF - 1)).astype(F32).astype(BF16)
        onehot = jnp.where(iota == key, one, zero)
        found = jnp.dot(table, onehot, preferred_element_type=F32)
        big = col // BLOCK
        side = (col // HALF) & 1
        which = (row + 1) * 24 + jnp.where(big < 8, side * 8 + big, 8 + side * 4 + big)
        got = [jnp.zeros((8, BLOCK), F32) for _ in range(fields)]
        for r in range(3):
            for t in range(3):
                hit = sub == which - (r * 24 + t * 8)
                for v in range(fields):
                    start = (r * fields + v) * 24 + t * 8
                    got[v] = jnp.where(hit, found[start : start + 8], got[v])
        for v in range(fields):
            acc[v] = acc[v] + got[v] * weight
    return [jnp.sum(a, axis=0, keepdims=True) for a in acc]


def advance_fast(table, k, row_ref, col_ref, weight_ref, new_ref, length, fields, blocks, real_blocks):
    new_ref[...] = jnp.zeros_like(new_ref)

    def body(b, carry):
        interp = pick_block(b, k, table, row_ref, col_ref, weight_ref, fields)
        point = b * BLOCK + lax.broadcasted_iota(jnp.int32, (1, BLOCK), 1)
        for v in range(fields):
            value = interp[v] + 0.5 * interp[(v + 1) % fields] * jnp.tanh(interp[(v + 2) % fields])
            new_ref[pl.ds(v * blocks + b, 1), :] = jnp.where(point < length, value, 0.0)
        return carry

    lax.fori_loop(0, real_blocks, body, 0)


GROUP = 16
MESH = pl.DeviceIdType.MESH


def mask_group(g, first, orders_ref, leg_ref, rows_j):
    degree = lax.broadcasted_iota(jnp.int32, (rows_j, leg_ref.shape[2]), 1)
    for pair in range(GROUP // 2):
        rows = slice(2 * pair * rows_j, 2 * (pair + 1) * rows_j)
        both = leg_ref[g, rows, :].astype(F32)
        parts = []
        for s in range(2):
            keep = degree >= orders_ref[first + g * GROUP + 2 * pair + s]
            parts.append(jnp.where(keep, both[s * rows_j : (s + 1) * rows_j], 0.0))
        leg_ref[g, rows, :] = jnp.concatenate(parts, axis=0).astype(BF16)


def forward_group(g, fields, rows_j, spec_ref, leg_ref, four_ref, square_ref):
    masked = leg_ref[g]
    state = spec_ref[g].reshape(fields * GROUP, spec_ref.shape[3])
    both = lax.dot_general(
        masked, jnp.concatenate([state, masked], axis=0), (((1,), (1,)), ((), ())),
        preferred_element_type=F32,
    )
    size = GROUP * rows_j
    width = fields * GROUP
    row = lax.broadcasted_iota(jnp.int32, (size, width), 0) // rows_j
    col = lax.broadcasted_iota(jnp.int32, (size, width), 1) % GROUP
    prod = jnp.where(row == col, both[:, :width], 0.0)
    four_ref[g] = jnp.sum(prod.reshape(GROUP, rows_j, width), axis=0)
    row = lax.broadcasted_iota(jnp.int32, (size, size), 0)
    col = lax.broadcasted_iota(jnp.int32, (size, size), 1)
    square = jnp.where(row // rows_j == col // rows_j, both[:, width:], 0.0)
    square_ref[g] = jnp.sum(square.reshape(GROUP, rows_j, size), axis=0)


def gram_of(square_ref, gram_ref, rows_j):
    groups, _, size = square_ref.shape
    row = lax.broadcasted_iota(jnp.int32, (size, size), 0)
    col = lax.broadcasted_iota(jnp.int32, (size, size), 1)
    swap = (row // rows_j == col % GROUP) & (row % rows_j == col // GROUP)
    turned = jnp.dot(
        square_ref[...].reshape(groups * rows_j, size), jnp.where(swap, 1.0, 0.0),
        preferred_element_type=F32, precision="highest",
    )
    gram_ref[...] = jnp.zeros_like(gram_ref)
    for h in range(groups):
        rows = turned[h * rows_j : (h + 1) * rows_j]
        for j in range(rows_j):
            gram_ref[j, :, h * GROUP : (h + 1) * GROUP] = rows[:, j * GROUP : (j + 1) * GROUP]


def inverse_group(g, fields, rows_j, coef_ref, leg_ref, out_ref):
    size = GROUP * rows_j
    row = lax.broadcasted_iota(jnp.int32, (size, fields * GROUP), 0) // rows_j
    col = lax.broadcasted_iota(jnp.int32, (size, fields * GROUP), 1) % GROUP
    tiled = jnp.concatenate([coef_ref[g]] * GROUP, axis=0)
    spread = jnp.where(row == col, tiled, 0.0).T.astype(BF16)
    out = jnp.dot(spread, leg_ref[g], preferred_element_type=F32)
    out_ref[g] = out.astype(BF16).reshape(out_ref.shape[1:])


def steps_kernel(
    steps, count, fields, blocks, real_blocks, slots,
    spec_hbm, leg_hbm, orders_ref, row_ref, col_ref, weight_ref, order_ref, len_ref, gauss_ref,
    out_hbm,
    spec_ref, leg_ref, four_ref, square_ref, vjs_ref, first_ref, gram_ref, load_sem, out_sem,
    cos_ref, sin_ref, fc_ref, fs_ref, ca_ref, sa_ref, spec_send, spec_recv, grid_send, grid_recv, tab_ref, coef_ref,
    new_ref, spec_ssem, spec_rsem, grid_ssem, grid_rsem, halo_ssem, halo_rsem,
):
    rows_j = leg_ref.shape[1] // GROUP
    groups = slots // GROUP

    def loads(g):
        slot_rows = pl.ds(pl.multiple_of(g * GROUP, GROUP), GROUP)
        return (
            pltpu.make_async_copy(leg_hbm.at[g], leg_ref.at[g], load_sem.at[0, g]),
            pltpu.make_async_copy(spec_hbm.at[:, slot_rows, :], spec_ref.at[g], load_sem.at[1, g]),
        )

    def store(g):
        slot_rows = pl.ds(pl.multiple_of(g * GROUP, GROUP), GROUP)
        return pltpu.make_async_copy(spec_ref.at[g], out_hbm.at[:, slot_rows, :], out_sem.at[g])

    for g in range(groups):
        for copy in loads(g):
            copy.start()
    tab_ref[...] = jnp.zeros_like(tab_ref)
    vjs_ref[...] = jnp.zeros_like(vjs_ref)
    grid_send[...] = jnp.zeros_like(grid_send)
    me = lax.axis_index("wave")
    peers = [lax.rem(me + d, count) for d in range(1, count)]
    barrier = pltpu.get_barrier_semaphore()
    for peer in peers:
        pl.semaphore_signal(barrier, inc=1, device_id={"wave": peer}, device_id_type=MESH)
    length = len_ref[me]
    orders = orders_ref[...]
    limit = jnp.minimum(orders.shape[1], (length - 1) // 2)
    fill_phases(orders, length, cos_ref, sin_ref)

    def forward(g, carry):
        for copy in loads(g):
            copy.wait()
        mask_group(g, me * slots, order_ref, leg_ref, rows_j)
        forward_group(g, fields, rows_j, spec_ref, leg_ref, four_ref, square_ref)
        return carry

    lax.fori_loop(0, groups, forward, 0, unroll=2)
    for h in range(groups):
        for v in range(fields):
            vjs_ref[v, :, h * GROUP : (h + 1) * GROUP] = four_ref[
                h, :, v * GROUP : (v + 1) * GROUP
            ]
    first_ref[...] = jnp.swapaxes(vjs_ref[...], 0, 1)
    pl.semaphore_wait(barrier, count - 1)

    def exchange(send, recv, ssem, rsem):
        copies = []
        for d, peer in enumerate(peers):
            copy = pltpu.make_async_remote_copy(
                src_ref=send.at[peer], dst_ref=recv.at[me], send_sem=ssem.at[d],
                recv_sem=rsem.at[d], device_id={"wave": peer}, device_id_type=MESH,
            )
            copy.start()
            copies.append(copy)
        return copies

    copies = exchange(first_ref, spec_recv.at[0], spec_ssem.at[0], spec_rsem.at[0])
    gram_of(square_ref, gram_ref, rows_j)
    active = jnp.where(orders < limit, 1.0, 0.0)
    build_table(cos_ref, sin_ref, active, fc_ref, fs_ref, ca_ref, sa_ref)
    grid_scale = 1.0 / jnp.sqrt(jnp.full((1, BLOCK), limit.astype(F32)))
    coef_scale = gauss_ref[0] * jnp.sqrt(2.0 / jnp.full(orders.shape, length.astype(F32)))
    cos_block = cos_ref[3 * RADIX : 3 * RADIX + blocks, :]
    sin_block = sin_ref[3 * RADIX : 3 * RADIX + blocks, :]
    rows = fields // 2 * 24
    for k in range(steps):
        source = first_ref if k == 0 else spec_send.at[k - 1]
        for copy in copies:
            copy.wait()
        spec_recv[k, me] = source[me]
        for i in range(count):
            coef_ref[:, i * slots : (i + 1) * slots] = spec_recv[k, i, :, :slots]
        own = grid_rows(
            coef_ref[...], cos_block, sin_block, fc_ref, fs_ref, length, grid_scale
        )
        tab_ref[k, 1] = own.astype(BF16)
        up = pltpu.make_async_remote_copy(
            src_ref=tab_ref.at[k, 1], dst_ref=tab_ref.at[k, 0], send_sem=halo_ssem.at[k, 0],
            recv_sem=halo_rsem.at[k, 0], device_id={"wave": lax.rem(me + 1, count)},
            device_id_type=MESH,
        )
        down = pltpu.make_async_remote_copy(
            src_ref=tab_ref.at[k, 1], dst_ref=tab_ref.at[k, 2], send_sem=halo_ssem.at[k, 1],
            recv_sem=halo_rsem.at[k, 1], device_id={"wave": lax.rem(me + count - 1, count)},
            device_id_type=MESH,
        )

        @pl.when(me < count - 1)
        def _():
            up.start()

        @pl.when(me > 0)
        def _():
            down.start()
            up.wait_recv()

        @pl.when(me < count - 1)
        def _():
            down.wait_recv()

        table = tab_ref[k].reshape(3 * rows, HALF)
        advance_fast(
            table, k, row_ref, col_ref, weight_ref, new_ref, length,
            fields // 2, blocks, real_blocks,
        )

        @pl.when(me < count - 1)
        def _():
            up.wait_send()

        @pl.when(me > 0)
        def _():
            down.wait_send()

        parts = analyse(new_ref, cos_block, sin_block, fc_ref, fs_ref, coef_scale)
        for v, part in enumerate(parts):
            coef_ref[v : v + 1, :] = part
        for i in range(count):
            grid_send[k, i, :, :slots] = coef_ref[:, i * slots : (i + 1) * slots]
        copies = exchange(grid_send.at[k], grid_recv.at[k], grid_ssem.at[k], grid_rsem.at[k])
        grid_recv[k, me] = grid_send[k, me]
        for copy in copies:
            copy.wait()
        if k + 1 < steps:
            mixed = []
            for v in range(fields):
                total = None
                for j in range(count):
                    term = gram_ref[j] * grid_recv[k, j, v : v + 1, :]
                    total = term if total is None else total + term
                mixed.append(total[None])
            spec_send[k] = jnp.swapaxes(jnp.concatenate(mixed, axis=0), 0, 1)
            copies = exchange(
                spec_send.at[k], spec_recv.at[k + 1], spec_ssem.at[k + 1], spec_rsem.at[k + 1]
            )
    last = jnp.swapaxes(grid_recv[steps - 1], 0, 1)
    for h in range(slots // GROUP):
        for v in range(fields):
            four_ref[h, :, v * GROUP : (v + 1) * GROUP] = last[v, :, h * GROUP : (h + 1) * GROUP]

    def inverse(g, carry):
        inverse_group(g, fields, rows_j, four_ref, leg_ref, spec_ref)
        store(g).start()
        return carry

    lax.fori_loop(0, groups, inverse, 0, unroll=2)
    for g in range(groups):
        store(g).wait()


def fused(spectrum, legendre, order_of_slot, reduced_length, gauss_weight, row, col, weight, count):
    slots, rows_j, degrees = legendre.shape
    fields = 2 * spectrum.shape[0]
    orders_total = order_of_slot.shape[0]
    steps, stencil, grid_width = row.shape[0], row.shape[2], row.shape[-1]
    real_blocks = grid_width // BLOCK
    blocks = padded_blocks(grid_width)
    groups = slots // GROUP
    size = GROUP * rows_j
    lanes = -(-slots // 128) * 128
    shape = (steps, count, fields, lanes)
    table_rows = fields // 2 * blocks
    out = pl.pallas_call(
        functools.partial(steps_kernel, steps, count, fields, blocks, real_blocks, slots),
        out_shape=jax.ShapeDtypeStruct((fields, slots, degrees), BF16),
        in_specs=[pl.BlockSpec(memory_space=pl.ANY)] * 2 + [VMEM_SPEC] * 4 + [SMEM_SPEC] * 3,
        out_specs=pl.BlockSpec(memory_space=pl.ANY),
        scratch_shapes=[
            pltpu.VMEM((groups, fields, GROUP, degrees), BF16),
            pltpu.VMEM((groups, size, degrees), BF16),
            pltpu.VMEM((groups, rows_j, fields * GROUP), F32),
            pltpu.VMEM((groups, rows_j, size), F32),
            pltpu.VMEM((fields, rows_j, lanes), F32),
            pltpu.VMEM((rows_j, fields, lanes), F32),
            pltpu.VMEM((rows_j, rows_j, lanes), F32),
            pltpu.SemaphoreType.DMA((2, groups)),
            pltpu.SemaphoreType.DMA((groups,)),
        ]
        + [pltpu.VMEM((3 * RADIX + blocks, orders_total), F32)] * 2
        + [pltpu.VMEM((BLOCK, orders_total), BF16)] * 2
        + [pltpu.VMEM((RADIX * RADIX, orders_total), F32)] * 2
        + [pltpu.VMEM(shape, F32)] * 4
        + [
            pltpu.VMEM((steps, 3, fields // 2 * 24, HALF), BF16),
            pltpu.VMEM((fields, orders_total), F32),
            pltpu.VMEM((table_rows, BLOCK), F32),
        ]
        + [pltpu.SemaphoreType.DMA((steps, count - 1))] * 4
        + [pltpu.SemaphoreType.DMA((steps, 2))] * 2,
        compiler_params=pltpu.CompilerParams(collective_id=0, has_side_effects=True),
        name="steps",
    )(
        spectrum.reshape(fields, slots, degrees),
        legendre.reshape(groups, size, degrees),
        order_of_slot.reshape(1, orders_total),
        row.reshape(steps, stencil, 1, grid_width),
        col.reshape(steps, stencil, 1, grid_width),
        weight.reshape(steps, stencil, 1, grid_width),
        order_of_slot, reduced_length, gauss_weight,
    )
    return out.reshape(spectrum.shape)


def per_device(
    spectrum,
    legendre,
    order_of_slot,
    reduced_length,
    gauss_weight,
    depart_row,
    depart_col,
    depart_weight,
):
    own_index = lax.axis_index("wave")
    count = lax.axis_size("wave")
    slot_count = legendre.shape[0]
    orders_total = order_of_slot.shape[0]
    variables, level_count = spectrum.shape[:2]
    assert level_count == 1
    steps = depart_row.shape[0]
    grid_width = depart_row.shape[-1]
    stencil = depart_row.shape[2]
    fields = variables
    real_blocks = grid_width // BLOCK
    blocks = padded_blocks(grid_width)

    fits = slot_count % GROUP == 0 and 2 * fields == 8 and real_blocks <= 12
    if fits and legendre.shape[1] == 8 and count == 8:
        return fused(
            spectrum, legendre, order_of_slot, reduced_length, gauss_weight,
            depart_row, depart_col, depart_weight, count,
        )

    length = lax.dynamic_index_in_dim(reduced_length, own_index, keepdims=False)
    own_orders = lax.dynamic_slice_in_dim(order_of_slot, own_index * slot_count, slot_count)
    degrees = jnp.arange(legendre.shape[2], dtype=jnp.int32)
    masked = jnp.where(
        degrees[None, None, :] >= own_orders[:, None, None], legendre, jnp.zeros((), BF16)
    )
    order_limit = jnp.minimum(orders_total, (length - 1) // 2)
    cos_rows, sin_rows = phase_rows(length, order_of_slot, blocks)
    active = (order_of_slot < order_limit).astype(F32)[None, :]
    fc, fs = pl.pallas_call(
        build_table,
        out_shape=[jax.ShapeDtypeStruct((BLOCK, orders_total), BF16)] * 2,
        in_specs=[VMEM_SPEC] * 3,
        out_specs=[VMEM_SPEC] * 2,
        scratch_shapes=[pltpu.VMEM((RADIX * RADIX, orders_total), F32)] * 2,
        name="table",
    )(cos_rows, sin_rows, active)
    length1 = length.reshape(1)
    grid_scale = (1.0 / jnp.sqrt(order_limit.astype(F32))).reshape(1)
    coef_scale = (gauss_weight[0] * jnp.sqrt(2.0 / length.astype(F32))).reshape(1)

    synth = pl.pallas_call(
        functools.partial(synth_kernel, blocks),
        out_shape=jax.ShapeDtypeStruct((fields * blocks, BLOCK), BF16),
        in_specs=[VMEM_SPEC] * 5 + [SMEM_SPEC] * 2,
        out_specs=VMEM_SPEC,
        name="synth",
    )
    grid_step = pl.pallas_call(
        functools.partial(grid_kernel, fields, blocks, real_blocks),
        out_shape=jax.ShapeDtypeStruct((2 * fields, orders_total), BF16),
        in_specs=[VMEM_SPEC] * 8 + [SMEM_SPEC] * 2,
        out_specs=VMEM_SPEC,
        scratch_shapes=[pltpu.VMEM((fields * blocks, BLOCK), F32)],
        name="grid_step",
    )
    spectral = spectrum.reshape(2 * fields, slot_count, -1)
    fourier = jnp.einsum("vsn,sjn->jvs", spectral, masked, preferred_element_type=F32)
    gram = jnp.einsum("sjn,skn->sjk", masked, masked, preferred_element_type=F32)
    forward = [(i, i + 1) for i in range(count - 1)]
    backward = [(i + 1, i) for i in range(count - 1)]
    for k in range(steps):
        gathered = lax.all_to_all(fourier.astype(BF16), "wave", split_axis=0, concat_axis=2, tiled=True)
        own = synth(
            gathered.reshape(2 * fields, orders_total), cos_rows, sin_rows, fc, fs, length1, grid_scale
        )
        low = lax.ppermute(own, "wave", forward)
        high = lax.ppermute(own, "wave", backward)
        coeffs = grid_step(
            jnp.concatenate([low, own, high], axis=0),
            depart_row[k].reshape(1, stencil, 1, grid_width),
            depart_col[k].reshape(1, stencil, 1, grid_width),
            depart_weight[k].reshape(1, stencil, 1, grid_width),
            cos_rows, sin_rows, fc, fs, length1, coef_scale,
        )
        returned = lax.all_to_all(
            coeffs.reshape(1, 2 * fields, orders_total), "wave", split_axis=2, concat_axis=0, tiled=True
        )
        if k + 1 < steps:
            fourier = jnp.einsum("jvs,sjk->kvs", returned.astype(F32), gram, precision="highest")
    final = jnp.einsum("jvs,sjn->vsn", returned, masked, preferred_element_type=F32).astype(BF16)
    return final.reshape(spectrum.shape)


def solution(mesh):
    placed = (
        P(None, "lev", None, "wave", None),
        P("wave", None, None),
        P(),
        P(),
        P("wave"),
        P(None, "lev", None, "wave", None),
        P(None, "lev", None, "wave", None),
        P(None, "lev", None, "wave", None),
    )
    return jax.shard_map(
        per_device,
        mesh=mesh,
        in_specs=placed,
        out_specs=P(None, "lev", None, "wave", None),
        check_vma=False,
    )
```
